32 devices in a mesh: dp: 8 (over z, y), fsdp: 4 (over x, core).
Axes of the slice: x: 2, y: 2, z: 4, core: 2. Of those that a mesh axis runs over, the one named last changes fastest.
Arguments:
- inputs: bfloat16 [64, 128, 768], P(('dp', 'fsdp')), may hold values from -6 to 6
- species: int32 [64], P(('dp', 'fsdp')), may hold values 0 or 1
- gene_ids: int32 [64, 128], P(('dp', 'fsdp')), may hold values from 0 to 35999, as said below
- cotangent: bfloat16 [64, 128, 768], P(('dp', 'fsdp')), may hold values from -6 to 6
- table: bfloat16 [2, 768], P(None, 'fsdp'), may hold values from -3 to 3
- w_query: bfloat16 [768, 768], P('fsdp'), may hold values from -0.3125 to 0.3125
- b_query: bfloat16 [768], P('fsdp'), may hold values from -2 to 2
- w_key: bfloat16 [768, 768], P('fsdp'), may hold values from -0.3125 to 0.3125
- w_value: bfloat16 [768, 768], P('fsdp'), may hold values from -0.21875 to 0.21875
- b_value: bfloat16 [768], P('fsdp'), may hold values from -0.59765625 to 0.59765625
- w_out: bfloat16 [768, 768], P('fsdp'), may hold values from -0.875 to 0.875
- b_out: bfloat16 [768], P('fsdp'), may hold values from -2 to 2
- gain_one: bfloat16 [768], P('fsdp'), may hold values from 0.5 to 1.5
- shift_one: bfloat16 [768], P('fsdp'), may hold values from -2 to 2
- w_up: bfloat16 [768, 3072], P('fsdp'), may hold values from -0.21875 to 0.21875
- b_up: bfloat16 [3072], P('fsdp'), may hold values from -2 to 2
- w_down: bfloat16 [3072, 768], P('fsdp'), may hold values from -0.109375 to 0.109375
- b_down: bfloat16 [768], P('fsdp'), may hold values from -2 to 2
- gain_two: bfloat16 [768], P('fsdp'), may hold values from 0.5 to 1.5
- shift_two: bfloat16 [768], P('fsdp'), may hold values from -2 to 2
Outputs:
- output: bfloat16 [64, 128, 768], P(('dp', 'fsdp'))
- input_grad: bfloat16 [64, 128, 768], P(('dp', 'fsdp'))
- grad_table: float32 [2, 768], P(None, 'fsdp')
- grad_w_query: float32 [768, 768], P('fsdp')
- grad_b_query: float32 [768], P('fsdp')
- grad_w_key: float32 [768, 768], P('fsdp')
- grad_w_value: float32 [768, 768], P('fsdp')
- grad_b_value: float32 [768], P('fsdp')
- grad_w_out: float32 [768, 768], P('fsdp')
- grad_b_out: float32 [768], P('fsdp')
- grad_gain_one: float32 [768], P('fsdp')
- grad_shift_one: float32 [768], P('fsdp')
- grad_w_up: float32 [768, 3072], P('fsdp')
- grad_b_up: float32 [3072], P('fsdp')
- grad_w_down: float32 [3072, 768], P('fsdp')
- grad_b_down: float32 [768], P('fsdp')
- grad_gain_two: float32 [768], P('fsdp')
- grad_shift_two: float32 [768], P('fsdp')
The draws below stay inside these ranges and needn't reach their ends.
Inputs may be any that keep to these rules, and one draw needn't show every extreme that they name: `gene_ids`: 0 marks a padding position; the live genes of a cell come first and are at least 32; the first cell has all 128 positions live.
All inputs are finite; a program needn't handle non-finite values. No bound on the sum of `species` on one device may be relied on, other than what follows from the above.
Results may differ from the reference program's by a relative error of at most 0.02.
The reference program's roundings to bfloat16 on the way count: a program that leaves them out, or rounds other values in their place, can miss the bound.
Values may be sent and summed in bfloat16 or wider, within the bound.
No kernel may reach another device: no remote copies, remote signals or barrier semaphores. Data moves between devices by JAX's collectives and lax.ppermute only.
A program may use at most 192 MiB of HBM per device.

```python
import math
import jax
import jax.numpy as jnp
from jax import lax

D = 768
HEADS = 12
HEAD_DIM = 64
FF = 3072
LEN = 128
GENE_IDS = 36000
CELLS = 64


def draw_gene_ids(key, part):
    key_lengths, key_genes = jax.random.split(jax.random.fold_in(key, 17))
    lengths = jax.random.randint(key_lengths, (CELLS,), LEN // 4, LEN + 1)
    lengths = lengths.at[0].set(LEN)
    positions = jnp.arange(LEN, dtype=jnp.int32)[None, :]
    gene_values = jax.random.randint(key_genes, (CELLS, LEN), 1, GENE_IDS)
    return jnp.where(positions < lengths[:, None], gene_values, 0).astype(jnp.int32)


def touch_ends(entries, own_key, low, high):
    extent = entries.shape
    index_at = [jax.random.randint(jax.random.fold_in(own_key, axis), (), 0, extent[axis]) for axis in range(len(extent))]
    entries = entries.at[tuple(index_at)].set(low)
    longest = extent.index(max(extent))
    index_at[longest] = (index_at[longest] + 1) % extent[longest]
    return entries.at[tuple(index_at)].set(high)


def strengthened(drawn, rng, source, target, shards_of, factor):
    def block_of(position):
        return (jnp.arange(drawn.shape[position]) // (drawn.shape[position] // shards_of)).reshape((-1,) + (1,) * (drawn.ndim - 1 - position))

    first = jax.random.permutation(rng, shards_of)[block_of(target)]
    other_side = (block_of(target) + shards_of // 2) % shards_of
    return jnp.where((block_of(source) == first) | (block_of(source) == other_side), factor * drawn, drawn)


def levels(own_key, extent, cuts, low, high):
    level, own = 1.0, jax.random.fold_in(own_key, 6)
    for axis_at, shards_of in cuts:
        draws = jnp.exp(jax.random.uniform(jax.random.fold_in(own, axis_at), (shards_of,), jnp.float32, low / len(cuts), high / len(cuts)))
        level = level * jnp.repeat(draws, extent[axis_at] // shards_of).reshape([-1 if axis == axis_at else 1 for axis in range(len(extent))])
    return level


def gaussian(rng, extent, spread, bound, cuts=(), kind=jnp.bfloat16):
    drawn = jax.random.normal(rng, extent, jnp.float32) * spread
    if len(cuts) > 0:
        drawn = levels(rng, extent, cuts, -0.22, 0.18) * drawn
    return jnp.clip(drawn, min=-bound, max=bound).astype(kind)


def noise_with(key, shape, scale, most, shards, heavy, held_as=jnp.bfloat16):
    array = scale * jax.random.normal(key, shape, jnp.float32)
    if shards:
        array = array * levels(key, shape, shards, -0.22, 0.18)
    return jnp.clip(strengthened(array, jax.random.fold_in(key, 3), *heavy), -most, most).astype(held_as)


def setup_inputs(seed: int = 0) -> dict:
    key_of = jax.random.split(jax.random.key(seed), 21)
    inputs = gaussian(key_of[0], (CELLS, LEN, D), 1.0, 6.0, ((0, 32),))
    species = touch_ends((jax.random.randint(key_of[1], (CELLS,), 0, 4) < 1).astype(jnp.int32), jax.random.fold_in(key_of[1], 1), 0, 1)
    gene_ids = draw_gene_ids(jax.random.fold_in(key_of[20], 71), 0)
    cotangent = noise_with(key_of[3], (CELLS, LEN, D), 1.0, 6.0, ((0, 32),), (0, 2, 32, 2.75))
    table = gaussian(key_of[4], (2, D), 0.5, 3.0, ((1, 4),))
    w_query = gaussian(key_of[5], (D, D), (D // 2) ** -0.5, 0.3125, ((0, 4),))
    b_query = gaussian(key_of[6], (D,), 0.3, 2.0, ((0, 4),))
    w_key = gaussian(key_of[7], (D, D), (D // 2) ** -0.5, 0.3125, ((0, 4),))
    w_value = gaussian(key_of[8], (D, D), D ** -0.5, 0.21875, ((0, 4),))
    b_value = gaussian(key_of[9], (D,), 0.1, 0.59765625, ((0, 4),))
    w_out = gaussian(key_of[10], (D, D), (D // 16) ** -0.5, 0.875, ((0, 4),))
    b_out = gaussian(key_of[11], (D,), 0.3, 2.0, ((0, 4),))
    gain_one = jnp.clip(1.0 + 0.1 * jax.random.normal(key_of[12], (D,), jnp.float32), 0.5, 1.5).astype(jnp.bfloat16)
    shift_one = gaussian(key_of[13], (D,), 0.3, 2.0, ((0, 4),))
    w_up = gaussian(key_of[14], (D, FF), D ** -0.5, 0.21875, ((0, 4),))
    b_up = gaussian(key_of[15], (FF,), 0.3, 2.0, ((0, 4),))
    w_down = gaussian(key_of[16], (FF, D), FF ** -0.5, 0.109375, ((0, 4),))
    b_down = gaussian(key_of[17], (D,), 0.3, 2.0, ((0, 4),))
    gain_two = jnp.clip(1.0 + 0.1 * jax.random.normal(key_of[18], (D,), jnp.float32), 0.5, 1.5).astype(jnp.bfloat16)
    shift_two = gaussian(key_of[19], (D,), 0.3, 2.0, ((0, 4),))
    return {"inputs": inputs, "species": species, "gene_ids": gene_ids, "cotangent": cotangent, "table": table, "w_query": w_query, "b_query": b_query, "w_key": w_key, "w_value": w_value, "b_value": b_value, "w_out": w_out, "b_out": b_out, "gain_one": gain_one, "shift_one": shift_one, "w_up": w_up, "b_up": b_up, "w_down": w_down, "b_down": b_down, "gain_two": gain_two, "shift_two": shift_two}


@jax.custom_vjp
def low(v):
    return lax.optimization_barrier(v.astype(jnp.bfloat16)).astype(jnp.float32)

@jax.custom_vjp
def low_back(v):
    return v

def low_keep(v):
    return (low(v), None)

def low_pass(kept, grad):
    return (grad,)

def back_keep(v):
    return (v, None)

def back_low(kept, grad):
    return (low(grad),)
low.defvjp(low_keep, low_pass)
low_back.defvjp(back_keep, back_low)
norm_eps = 1e-12
masked_score = -1e+30
highest = lax.Precision.HIGHEST

def layer_norm(residual, gain, shift):
    average = lax.optimization_barrier(jnp.mean(residual, axis=-1, keepdims=True))
    centred = residual - average
    inverse = lax.rsqrt(lax.optimization_barrier(jnp.mean(centred * centred, axis=-1, keepdims=True)) + norm_eps)
    return centred * inverse * gain + shift

def attend(query_rows, key_rows, value_rows, live_keys):
    group_cells = query_rows.shape[0]
    block_rows = min(512, LEN)
    block_count = LEN // block_rows
    score_scale = HEAD_DIM ** (-0.5)
    blocks = query_rows.reshape(group_cells, block_count, block_rows, HEADS, HEAD_DIM).transpose(1, 0, 2, 3, 4)

    def one_block(block_part):
        scores = jnp.einsum('cqhe,ckhe->chqk', block_part, key_rows, precision=highest) * score_scale
        scores = low_back(scores)
        scores = jnp.where(live_keys[:, None, None, :], scores, masked_score)
        soft = jax.nn.softmax(scores, axis=-1)
        return jnp.einsum('chqk,ckhe->cqhe', low(soft), value_rows, precision=highest)
    attended = lax.map(jax.checkpoint(one_block), blocks)
    return attended.transpose(1, 0, 2, 3, 4).reshape(group_cells, LEN, HEADS * HEAD_DIM)

def forward(inputs, onehot, live_keys, table, w_query, b_query, w_key, w_value, b_value, w_out, b_out, gain_one, shift_one, w_up, b_up, w_down, b_down, gain_two, shift_two):
    group_cells = inputs.shape[0]
    offsets = jnp.dot(onehot, table, precision=highest)
    summed = inputs + offsets[:, None, :]
    summed_low = low(summed)
    query_rows = low_back(low(jnp.einsum('cld,de->cle', summed_low, w_query, precision=highest) + b_query))
    key_rows = low_back(low(jnp.einsum('cld,de->cle', summed_low, w_key, precision=highest)))
    value_rows = low_back(low(jnp.einsum('cld,de->cle', summed_low, w_value, precision=highest) + b_value))
    split_shape = (group_cells, LEN, HEADS, HEAD_DIM)
    attended = attend(query_rows.reshape(split_shape), key_rows.reshape(split_shape), value_rows.reshape(split_shape), live_keys)
    attended = low_back(low(attended))
    branch = low_back(jnp.einsum('cld,de->cle', attended, w_out, precision=highest) + b_out)
    residual = summed + branch
    normed = layer_norm(residual, gain_one, shift_one)
    up_input = low_back(jnp.einsum('cld,df->clf', low(normed), w_up, precision=highest) + b_up)
    active = low(jax.nn.gelu(up_input, approximate=False))
    branch_two = low_back(jnp.einsum('clf,fd->cld', active, w_down, precision=highest) + b_down)
    return layer_norm(normed + branch_two, gain_two, shift_two)

def reference(inputs, species, gene_ids, cotangent, table, w_query, b_query, w_key, w_value, b_value, w_out, b_out, gain_one, shift_one, w_up, b_up, w_down, b_down, gain_two, shift_two):
    weights = tuple((weight_arg.astype(jnp.float32) for weight_arg in (table, w_query, b_query, w_key, w_value, b_value, w_out, b_out, gain_one, shift_one, w_up, b_up, w_down, b_down, gain_two, shift_two)))
    group_cells = math.gcd(CELLS, max(1, 4096 // LEN))
    group_count = CELLS // group_cells
    onehot = (species[:, None] == jnp.arange(2, dtype=jnp.int32)[None, :]).astype(jnp.float32)
    live_keys = gene_ids != 0

    def regroup(whole_array):
        return whole_array.reshape((group_count, group_cells) + whole_array.shape[1:])

    def one_group(totals, pieces):
        input_part, onehot_part, live_part, cotangent_part = pieces

        def forward_group(input_rows, *params):
            return forward(input_rows, onehot_part, live_part, *params)
        output_part, pullback = jax.vjp(forward_group, input_part.astype(jnp.float32), *weights)
        gradients = pullback(cotangent_part.astype(jnp.float32))
        totals = tuple((total_part + new_part for total_part, new_part in zip(totals, gradients[1:])))
        return (totals, (output_part.astype(jnp.bfloat16), gradients[0].astype(jnp.bfloat16)))
    zero_grads = tuple((jnp.zeros(weight_arg.shape, jnp.float32) for weight_arg in weights))
    totals, (output, input_grad) = lax.scan(one_group, zero_grads, (regroup(inputs), regroup(onehot), regroup(live_keys), regroup(cotangent)))
    return (output.reshape(inputs.shape), input_grad.reshape(inputs.shape), totals[0], totals[1], totals[2], totals[3], totals[4], totals[5], totals[6], totals[7], totals[8], totals[9], totals[10], totals[11], totals[12], totals[13], totals[14], totals[15])
```

```python
from functools import partial

import jax
import jax.numpy as jnp
from jax import lax
from jax.experimental import pallas as pl
from jax.experimental.pallas import tpu as pltpu
from jax.sharding import PartitionSpec as P

HEAD_DIM = 64
norm_eps = 1e-12
masked_score = -1e30
f32 = jnp.float32
bf16 = jnp.bfloat16

BQ, BV, BO, G1, S1, BD, G2, S2, TB, BU = 0, 1, 2, 3, 4, 5, 6, 7, 8, 10
VEC_ROWS = 16
COST = 1024
ATTEND_COST = 1024
VMEM_LIMIT = 56 * 1024 * 1024


def dot(a, b):
    return jnp.dot(a, b, preferred_element_type=f32)


def dot_nt(a, b):
    return lax.dot_general(a, b, (((1,), (1,)), ((), ())), preferred_element_type=f32)


def dot_tn(a, b):
    return lax.dot_general(a, b, (((0,), (0,)), ((), ())), preferred_element_type=f32)


def swap(x, axis, distance):
    count = lax.axis_size(axis)
    with jax.named_scope(f"swap_{axis}{distance}"):
        return lax.ppermute(x, axis, [(i, i ^ distance) for i in range(count)])


def half_columns(x, bit):
    width = x.shape[1] // 2
    return lax.dynamic_slice_in_dim(x, bit * width, width, 1)


def tie(x, *others):
    return lax.optimization_barrier((x,) + others)[0]


def piece_slots(where_ref, width, count):
    f, y = where_ref[0], where_ref[1]
    if count == 4:
        return tuple((f ^ n, 0, width) for n in range(4))
    half = width // 2
    low = pl.multiple_of(y * half, 128)
    high = pl.multiple_of((1 - y) * half, 128)
    return (
        (f, 0, width),
        (f ^ 1, 0, width),
        (f ^ 2, low, half),
        (f ^ 2, high, half),
        (f ^ 3, low, half),
        (f ^ 3, high, half),
    )


def start_rows(pieces, where_ref, first_row, rows, width, target, sems, base):
    copies = []
    for n, (piece, (shard, col, cols)) in enumerate(zip(pieces, piece_slots(where_ref, width, len(pieces)))):
        copy = pltpu.make_async_copy(
            piece.at[pl.ds(first_row, rows), :],
            target.at[pl.ds(pl.multiple_of(shard * rows, 8), rows), pl.ds(col, cols)],
            sems.at[base + n],
        )
        copy.start()
        copies.append(copy)
    return copies


def wait_all(copies):
    for copy in copies:
        copy.wait()


def call(kernel, out_shapes, n_smem, n_vmem, n_any, scratch, name, cost=COST):
    return pl.pallas_call(
        kernel,
        out_shape=out_shapes,
        in_specs=[pl.BlockSpec(memory_space=pltpu.SMEM)] * n_smem
        + [pl.BlockSpec(memory_space=pltpu.VMEM)] * n_vmem
        + [pl.BlockSpec(memory_space=pl.ANY)] * n_any,
        out_specs=jax.tree.map(lambda _: pl.BlockSpec(memory_space=pltpu.VMEM), out_shapes),
        scratch_shapes=scratch,
        compiler_params=pltpu.CompilerParams(vmem_limit_bytes=VMEM_LIMIT),
        cost_estimate=pl.CostEstimate(flops=cost, bytes_accessed=cost, transcendentals=0),
        name=name,
    )


def sds(shape, dtype):
    return jax.ShapeDtypeStruct(shape, dtype)


def norm_forward(residual):
    average = jnp.mean(residual, axis=-1, keepdims=True)
    centred = residual - average
    inverse = lax.rsqrt(jnp.mean(centred * centred, axis=-1, keepdims=True) + norm_eps)
    return centred * inverse, inverse


def norm_backward(grad_out, normal, inverse, gain):
    scaled = grad_out * gain
    first = jnp.mean(scaled, axis=-1, keepdims=True)
    second = jnp.mean(scaled * normal, axis=-1, keepdims=True)
    return inverse * (scaled - first - normal * second)


def column_sum(x):
    return jnp.sum(x, axis=0, keepdims=True)


def head_mask(h, rows):
    lane = lax.broadcasted_iota(jnp.int32, (rows, 2 * HEAD_DIM), 1)
    return (lane // HEAD_DIM) == h


def soft_rows(q_pair, k_pair, dead, mask):
    scale = HEAD_DIM ** (-0.5)
    q_head = jnp.where(mask, q_pair, jnp.zeros_like(q_pair))
    scores = dot_nt(q_head, k_pair) * scale
    scores = jnp.where(dead, masked_score, scores)
    expo = jnp.exp(scores - jnp.max(scores, axis=-1, keepdims=True))
    return expo / jnp.sum(expo, axis=-1, keepdims=True)


def pack_kernel(where_ref, q_ref, k_ref, v_ref, o_ref, up_ref, *refs):
    vectors, table_ref, b_up_ref = refs[:TB], refs[TB], refs[TB + 1]
    all_ref, half_ref, half_up_ref, spread = refs[TB + 2 :]
    rows, width = q_ref.shape
    f, y = where_ref[0], where_ref[1]
    half = half_ref.shape[1]
    half_up = half_up_ref.shape[1]
    cols = pl.ds(pl.multiple_of(y * half, 128), half)
    for m, ref in enumerate((q_ref, k_ref, v_ref, o_ref)):
        at = slice(m * rows, (m + 1) * rows)
        half_ref[at, :] = ref[:, cols]
        all_ref[at, :] = ref[...]
    half_up_ref[...] = up_ref[:, pl.ds(pl.multiple_of(y * half_up, 128), half_up)]
    spread[...] = jnp.zeros(spread.shape, f32)
    table = table_ref[...].astype(f32)
    for k in range(4):

        @pl.when(f == k)
        def _():
            mine = slice(k * rows, (k + 1) * rows)
            for n, ref in enumerate(vectors):
                spread[n : n + 1, mine] = ref[...].astype(f32).reshape(1, rows)
            spread[TB : TB + 2, mine] = table
            spread[BU + k : BU + k + 1, :] = b_up_ref[...].astype(f32).reshape(1, width)

    all_ref[4 * rows :, :] = spread[...].astype(bf16)
    half_ref[4 * rows :, :] = spread[:, cols].astype(bf16)


def put_blocks(value, f, blocks, targets, at):
    rows = value.shape[1] // 4
    for i in range(4):
        blocks[i] = value[:, i * rows : (i + 1) * rows]
    for n, target in enumerate(targets):
        target[at] = blocks[f ^ n]
        target[at + 1] = blocks[f ^ 2 ^ n]


def attend_kernel(
    where_ref,
    species_ref,
    x_ref,
    ids_ref,
    *refs,
    length,
):
    pieces = refs[:6]
    (
        q_ref,
        k_ref,
        v_ref,
        own_ref,
        share_ref,
        n1_ref,
        inv_ref,
        low_ref,
        low_own_ref,
        low_share_ref,
        vec_ref,
        wbuf,
        vbuf,
        abuf,
        blocks,
        sems,
    ) = refs[6:]
    f = where_ref[0]
    tokens, width = x_ref.shape
    cells = tokens // length
    rows = width // 4
    copies = []
    for m in range(4):
        copies.append(
            start_rows(pieces, where_ref, m * rows, rows, width, wbuf.at[m], sems, 6 * m)
        )
    vec_copies = start_rows(pieces, where_ref, 4 * rows, VEC_ROWS, width, vbuf, sems, 24)
    wait_all(vec_copies)
    vec = vbuf[0:VEC_ROWS, :].astype(f32)
    for i in range(1, 4):
        vec = vec + vbuf[i * VEC_ROWS : (i + 1) * VEC_ROWS, :].astype(f32)
    vec_ref[...] = vec
    summed = []
    for c in range(cells):
        offset = jnp.where(species_ref[c] == 1, vec[TB + 1 : TB + 2, :], vec[TB : TB + 1, :])
        summed.append(x_ref[c * length : (c + 1) * length, :].astype(f32) + offset)
    summed = jnp.concatenate(summed, axis=0)
    summed_low = summed.astype(bf16)
    put_blocks(summed_low, f, blocks, (own_ref, share_ref), 2)
    wait_all(copies[0])
    q_ref[...] = (dot(summed_low, wbuf[0]) + vec[BQ : BQ + 1, :]).astype(bf16)
    wait_all(copies[1])
    k_ref[...] = dot(summed_low, wbuf[1]).astype(bf16)
    wait_all(copies[2])
    v_ref[...] = (dot(summed_low, wbuf[2]) + vec[BV : BV + 1, :]).astype(bf16)
    pair = 2 * HEAD_DIM
    masks = [head_mask(h, length) for h in range(2)]
    for c in range(cells):
        at = slice(c * length, (c + 1) * length)
        dead = jnp.broadcast_to(ids_ref[c : c + 1, :], (length, length)) == 0
        for p in range(width // pair):
            cols = slice(p * pair, (p + 1) * pair)
            q_pair, k_pair, v_pair = q_ref[at, cols], k_ref[at, cols], v_ref[at, cols]
            total = None
            for h in range(2):
                soft = soft_rows(q_pair, k_pair, dead, masks[h]).astype(bf16)
                part = dot(soft, jnp.where(masks[h], v_pair, jnp.zeros_like(v_pair)))
                total = part if total is None else total + part
            abuf[at, cols] = total.astype(bf16)
    attended = abuf[...]
    put_blocks(attended, f, blocks, (own_ref, share_ref), 0)
    wait_all(copies[3])
    branch = dot(attended, wbuf[3]) + vec[BO : BO + 1, :]
    normal, inverse = norm_forward(summed + branch)
    n1_ref[...] = normal
    inv_ref[...] = jnp.broadcast_to(inverse, inv_ref.shape)
    low = (normal * vec[G1 : G1 + 1, :] + vec[S1 : S1 + 1, :]).astype(bf16)
    low_ref[...] = low
    put_blocks(low, f, blocks, (low_own_ref, low_share_ref), 0)


def up_kernel(where_ref, low_ref, vec_ref, *refs):
    pieces = refs[:6]
    act_ref, own_ref, near_ref, across_ref, slope_ref, wbuf, sems = refs[6:]
    f = where_ref[0]
    hidden = wbuf.shape[1]
    rows = wbuf.shape[0] // 4
    block = hidden // 4
    wait_all(start_rows(pieces, where_ref, 0, rows, hidden, wbuf, sems, 0))
    low = low_ref[...]
    for j in range(4):
        up = dot(low, wbuf[:, j * block : (j + 1) * block]) + vec_ref[BU + j : BU + j + 1, :]
        half_cdf = 0.5 * (1.0 + lax.erf(up * (0.5**0.5)))
        density = jnp.exp(-0.5 * up * up) * 0.3989422804014327
        act_ref[j] = (up * half_cdf).astype(bf16)
        slope_ref[j] = half_cdf + up * density
    own_ref[...] = act_ref[f]
    near_ref[...] = act_ref[f ^ 1]
    across_ref[0] = act_ref[f ^ 2]
    across_ref[1] = act_ref[f ^ 3]


def down_kernel(where_ref, act_ref, n1_ref, vec_ref, cot_ref, *refs):
    pieces = refs[:4]
    out_ref, gsec_ref, glow_ref, sm_ref, wbuf, sems = refs[4:]
    rows = wbuf.shape[0] // 4
    width = wbuf.shape[1]
    copies = start_rows(pieces, where_ref, 0, rows, width, wbuf, sems, 0)
    vec = vec_ref[...]
    wait_all(copies)
    branch = None
    for j in range(4):
        part = dot(act_ref[j], wbuf[j * rows : (j + 1) * rows, :])
        branch = part if branch is None else branch + part
    normed = n1_ref[...] * vec[G1 : G1 + 1, :] + vec[S1 : S1 + 1, :]
    normal, inverse = norm_forward(normed + (branch + vec[BD : BD + 1, :]))
    gain = vec[G2 : G2 + 1, :]
    out_ref[...] = (normal * gain + vec[S2 : S2 + 1, :]).astype(bf16)
    cot = cot_ref[...].astype(f32)
    grad = norm_backward(cot, normal, inverse, gain)
    gsec_ref[...] = grad
    low = grad.astype(bf16)
    glow_ref[...] = low
    sm_ref[0:1, :] = column_sum(cot * normal)
    sm_ref[1:2, :] = column_sum(cot)
    sm_ref[2:3, :] = column_sum(low.astype(f32))
    sm_ref[3:8, :] = jnp.zeros((5, width), f32)


def near_up_kernel(where_ref, own_ref, got_ref, *refs):
    rights, got_rights, outs = refs[:4], refs[4:8], refs[8:]
    block = rights[0].shape[1]
    for slot, out in ((1, outs[0]), (0, outs[1])):
        for j in range(4):
            total = dot_tn(own_ref[slot], rights[j][...]) + dot_tn(got_ref[slot], got_rights[j][...])
            out[:, j * block : (j + 1) * block] = total.astype(bf16)


def near_attn_kernel(where_ref, own_ref, got_ref, *refs):
    rights, got_rights = refs[:4], refs[4:8]
    send_ref, keep_ref, send_y_ref, keep_y_ref = refs[8:]
    y = where_ref[1]
    rows = own_ref.shape[2]

    def block(left, n):
        return dot_tn(own_ref[left], rights[n][...]) + dot_tn(got_ref[left], got_rights[n][...])

    for slot, ref in ((1, send_ref), (0, keep_ref)):
        ref[0:rows, :] = block(slot, 0).astype(bf16)
        ref[rows : 2 * rows, :] = block(2 + slot, 1).astype(bf16)
    for ref, first in ((send_y_ref, 1 - y), (keep_y_ref, y)):
        right = jnp.where(first == 0, rights[2][...], rights[3][...])
        got_right = jnp.where(first == 0, got_rights[2][...], got_rights[3][...])
        for slot in (0, 1):
            total = dot_tn(own_ref[2 + slot], right) + dot_tn(got_ref[2 + slot], got_right)
            ref[slot] = total.astype(bf16)


def down_grad_kernel(where_ref, *refs):
    lefts, rights, outs = refs[:4], refs[4:8], refs[8:]
    z = where_ref[2]
    rows = outs[0].shape[0]
    for half, out in ((1 - z, outs[0]), (z, outs[1])):
        cols = pl.ds(pl.multiple_of(half * rows, 128), rows)
        total = None
        for n, (left, right) in enumerate(zip(lefts, rights)):
            part = dot_tn(left[0, :, cols] if n == 2 else left[:, cols], right[...])
            total = part if total is None else total + part
        out[...] = total.astype(bf16)


def hidden_back_kernel(where_ref, glow_ref, slope_ref, *refs):
    pieces = refs[:4]
    guis, sm_ref, wbuf, sems = refs[4:8], refs[8], refs[9], refs[10]
    rows = wbuf.shape[0] // 4
    width = wbuf.shape[1]
    wait_all(start_rows(pieces, where_ref, 0, rows, width, wbuf, sems, 0))
    glow = glow_ref[...]
    for j in range(4):
        grad = dot_nt(glow, wbuf[j * rows : (j + 1) * rows, :]) * slope_ref[j]
        low = grad.astype(bf16)
        guis[j][...] = low
        sm_ref[j : j + 1, :] = column_sum(low.astype(f32))
    sm_ref[4:8, :] = jnp.zeros((4, rows), f32)


def norm_back_kernel(where_ref, gsec_ref, n1_ref, inv_ref, vec_ref, *refs):
    guis, pieces, attn_pieces = refs[:4], refs[4:10], refs[10:16]
    gres_ref, gbr_ref, gatt_ref, sm_ref, wbuf, obuf, sems = refs[16:]
    rows = wbuf.shape[0] // 4
    hidden = wbuf.shape[1]
    width = obuf.shape[1]
    copies = start_rows(pieces, where_ref, 0, rows, hidden, wbuf, sems, 0)
    out_copies = start_rows(attn_pieces, where_ref, 3 * rows, rows, width, obuf, sems, 6)
    wait_all(copies)
    block = hidden // 4
    grad_normed = gsec_ref[...]
    for j in range(4):
        grad_normed = grad_normed + dot_nt(guis[j][...], wbuf[:, j * block : (j + 1) * block])
    normal = n1_ref[...]
    grad = norm_backward(grad_normed, normal, inv_ref[:, 0:1], vec_ref[G1 : G1 + 1, :])
    gres_ref[...] = grad
    low = grad.astype(bf16)
    gbr_ref[...] = low
    sm_ref[0:1, :] = column_sum(grad_normed * normal)
    sm_ref[1:2, :] = column_sum(grad_normed)
    sm_ref[2:3, :] = column_sum(low.astype(f32))
    sm_ref[3:8, :] = jnp.zeros((5, width), f32)
    wait_all(out_copies)
    gatt_ref[...] = dot_nt(low, obuf[...]).astype(bf16)


def attend_back_kernel(q_ref, k_ref, v_ref, gatt_ref, ids_ref, gq_ref, gk_ref, gv_ref, *, length):
    tokens, width = q_ref.shape
    cells = tokens // length
    scale = HEAD_DIM ** (-0.5)
    pair = 2 * HEAD_DIM
    masks = [head_mask(h, length) for h in range(2)]
    for c in range(cells):
        at = slice(c * length, (c + 1) * length)
        dead = jnp.broadcast_to(ids_ref[c : c + 1, :], (length, length)) == 0
        for p in range(width // pair):
            cols = slice(p * pair, (p + 1) * pair)
            q_pair, k_pair, v_pair = q_ref[at, cols], k_ref[at, cols], v_ref[at, cols]
            g_pair = gatt_ref[at, cols]
            zero = jnp.zeros_like(q_pair)
            gq = gk = gv = jnp.zeros((length, pair), f32)
            for h in range(2):
                mask = masks[h]
                soft = soft_rows(q_pair, k_pair, dead, mask)
                g_head = jnp.where(mask, g_pair, zero)
                grad_soft = dot_nt(g_head, v_pair)
                inner = jnp.sum(soft * grad_soft, axis=-1, keepdims=True)
                grad_scores = (soft * (grad_soft - inner)).astype(bf16)
                gv = gv + dot_tn(soft.astype(bf16), g_head)
                gq = gq + dot(grad_scores, jnp.where(mask, k_pair, zero))
                gk = gk + dot_tn(grad_scores, jnp.where(mask, q_pair, zero))
            gq_ref[at, cols] = (gq * scale).astype(bf16)
            gk_ref[at, cols] = (gk * scale).astype(bf16)
            gv_ref[at, cols] = gv.astype(bf16)


def input_back_kernel(
    where_ref, species_ref, gres_ref, gq_ref, gk_ref, gv_ref, sm2_ref, smu_ref, sm1_ref, *refs,
    length,
):
    pieces = refs[:6]
    gin_ref, sm_ref, wbuf, sems = refs[6:]
    tokens, width = gres_ref.shape
    rows = width // 4
    copies = [
        start_rows(pieces, where_ref, m * rows, rows, width, wbuf.at[m], sems, 6 * m)
        for m in range(3)
    ]
    sm_ref[BQ : BQ + 1, :] = column_sum(gq_ref[...].astype(f32))
    sm_ref[BV : BV + 1, :] = column_sum(gv_ref[...].astype(f32))
    sm_ref[BO : BO + 1, :] = sm1_ref[2:3, :]
    sm_ref[G1 : G1 + 2, :] = sm1_ref[0:2, :]
    sm_ref[BD : BD + 1, :] = sm2_ref[2:3, :]
    sm_ref[G2 : G2 + 2, :] = sm2_ref[0:2, :]
    sm_ref[BU : BU + 4, :] = smu_ref[0:4, :]
    sm_ref[BU + 4 : VEC_ROWS, :] = jnp.zeros((VEC_ROWS - BU - 4, width), f32)
    total = gres_ref[...]
    for m, grad in enumerate((gq_ref, gk_ref, gv_ref)):
        wait_all(copies[m])
        total = total + dot_nt(grad[...], wbuf[m])
    gin_ref[...] = total.astype(bf16)
    for s in range(2):
        row = jnp.zeros((1, width), f32)
        for c in range(tokens // length):
            cell = column_sum(total[c * length : (c + 1) * length, :])
            row = row + jnp.where(species_ref[c] == s, cell, jnp.zeros_like(cell))
        sm_ref[TB + s : TB + s + 1, :] = row


def half_rows(x, bit):
    rows = x.shape[-2] // 2
    return lax.dynamic_slice_in_dim(x, bit * rows, rows, x.ndim - 2)


def add(a, b):
    return (a.astype(f32) + b.astype(f32)).astype(bf16)


def scatter_cells(keep, got, dp_index, steps):
    for step in steps:
        bit = (dp_index >> step) & 1
        sent = add(half_rows(keep, 1 - bit), half_rows(got, 1 - bit))
        keep = add(half_rows(keep, bit), half_rows(got, bit))
        got = swap(sent, "dp", 1 << step)
    return keep, got


def gather_cells(total, dp_index, order):
    total = add(total, swap(total, "dp", 1 << order[-1]))
    for step in reversed(order[:-1]):
        bit = (dp_index >> step) & 1
        other = swap(total, "dp", 1 << step)
        total = jnp.where(
            bit == 0,
            jnp.concatenate([total, other], axis=0),
            jnp.concatenate([other, total], axis=0),
        )
    return total


def reduce_cells(keep, got, dp_index, order, done=0):
    return gather_cells(
        add(*scatter_cells(keep, got, dp_index, order[done:-1])), dp_index, order
    )


def local(
    inputs,
    species,
    gene_ids,
    cotangent,
    table,
    w_query,
    b_query,
    w_key,
    w_value,
    b_value,
    w_out,
    b_out,
    gain_one,
    shift_one,
    w_up,
    b_up,
    w_down,
    b_down,
    gain_two,
    shift_two,
):
    cells, length, width = inputs.shape
    tokens = cells * length
    rows = w_query.shape[0]
    hidden = w_up.shape[1]
    shard_hidden = w_down.shape[0]
    shards = lax.axis_size("fsdp")
    f = lax.axis_index("fsdp")
    d = lax.axis_index("dp")
    y_bit = d & 1
    where = jnp.stack([f, y_bit, (d >> 1) & 1]).astype(jnp.int32)
    order = tuple(range((lax.axis_size("dp") - 1).bit_length()))
    other_order = (1, 0) + order[2:]

    packed_rows = shards * rows + VEC_ROWS
    packed, half, half_up = call(
        pack_kernel,
        (
            sds((packed_rows, width), bf16),
            sds((packed_rows, width // 2), bf16),
            sds((rows, hidden // 2), bf16),
        ),
        1,
        7 + TB,
        0,
        [pltpu.VMEM((VEC_ROWS, width), f32)],
        "pack",
    )(
        where,
        w_query,
        w_key,
        w_value,
        w_out,
        w_up,
        b_query,
        b_value,
        b_out,
        gain_one,
        shift_one,
        b_down,
        gain_two,
        shift_two,
        table,
        b_up,
    )
    across = swap(half, "fsdp", 2)
    relayed = swap(across, "dp", 1)
    attn = (
        packed,
        swap(packed, "fsdp", 1),
        across,
        relayed,
        swap(across, "fsdp", 1),
        swap(relayed, "fsdp", 1),
    )
    across_up = swap(tie(half_up, across), "fsdp", 2)
    relayed_up = swap(across_up, "dp", 1)
    up = (
        w_up,
        swap(w_up, "fsdp", 1),
        across_up,
        relayed_up,
        swap(across_up, "fsdp", 1),
    )
    across_down = swap(tie(w_down, across_up), "fsdp", 2)

    x_rows = inputs.reshape(tokens, width)
    cot_rows = cotangent.reshape(tokens, width)
    flat_low = sds((tokens, width), bf16)
    flat = sds((tokens, width), f32)
    small = sds((8, width), f32)
    q, k, v, own_attn, share_attn, n1, inv1, low, low_own, low_share, vec = call(
        partial(attend_kernel, length=length),
        (
            flat_low,
            flat_low,
            flat_low,
            sds((4, tokens, rows), bf16),
            sds((4, tokens, rows), bf16),
            flat,
            sds((tokens, 128), f32),
            flat_low,
            sds((2, tokens, rows), bf16),
            sds((2, tokens, rows), bf16),
            sds((VEC_ROWS, width), f32),
        ),
        2,
        2,
        6,
        [
            pltpu.VMEM((4, width, width), bf16),
            pltpu.VMEM((4 * VEC_ROWS, width), bf16),
            pltpu.VMEM((tokens, width), bf16),
            pltpu.VMEM((4, tokens, rows), bf16),
            pltpu.SemaphoreType.DMA((30,)),
        ],
        "attend",
        ATTEND_COST,
    )(where, species, x_rows, gene_ids, *attn)
    up += (swap(tie(relayed_up, q), "fsdp", 1),)
    act, act_own, act_near, act_across, slope = call(
        up_kernel,
        (
            sds((shards, tokens, shard_hidden), bf16),
            *(sds((tokens, shard_hidden), bf16),) * 2,
            sds((2, tokens, shard_hidden), bf16),
            sds((shards, tokens, shard_hidden), f32),
        ),
        1,
        2,
        6,
        [pltpu.VMEM((width, hidden), bf16), pltpu.SemaphoreType.DMA((6,))],
        "up",
    )(where, low, vec, *up)
    down = (
        w_down,
        swap(w_down, "fsdp", 1),
        across_down,
        swap(tie(across_down, act_own), "fsdp", 1),
    )
    output, gsec, glow, sm2 = call(
        down_kernel,
        (flat_low, flat, flat_low, small),
        1,
        4,
        4,
        [pltpu.VMEM((hidden, width), bf16), pltpu.SemaphoreType.DMA((4,))],
        "down",
    )(where, act, n1, vec, cot_rows, *down)
    act_got = swap(act_across, "fsdp", 2)
    glow_across = swap(glow, "fsdp", 2)
    *guis, smu = call(
        hidden_back_kernel,
        (*(sds((tokens, shard_hidden), bf16),) * 4, sds((8, shard_hidden), f32)),
        1,
        2,
        4,
        [pltpu.VMEM((hidden, width), bf16), pltpu.SemaphoreType.DMA((4,))],
        "hidden_back",
    )(where, glow, slope, *down)
    guis_got = [swap(part, "fsdp", 1) for part in guis]
    gres, gbr, gatt, sm1 = call(
        norm_back_kernel,
        (flat, flat_low, flat_low, small),
        1,
        8,
        12,
        [
            pltpu.VMEM((width, hidden), bf16),
            pltpu.VMEM((width, width), bf16),
            pltpu.SemaphoreType.DMA((12,)),
        ],
        "norm_back",
    )(where, gsec, n1, inv1, vec, *guis, *up, *attn)
    act_all = (
        act_own,
        swap(tie(act_near, gbr), "fsdp", 1),
        act_got,
        swap(tie(act_got, gbr)[1], "fsdp", 1),
    )
    glow_all = (
        glow,
        swap(tie(glow, gbr), "fsdp", 1),
        glow_across,
        swap(tie(glow_across, gbr), "fsdp", 1),
    )
    send_up, keep_up = call(
        near_up_kernel, (sds((rows, hidden), bf16),) * 2, 1, 10, 0, [], "near_up"
    )(tie(where, gbr), low_own, swap(low_share, "fsdp", 1), *guis, *guis_got)
    got_up = swap(send_up, "fsdp", 2)
    down_half = sds((shard_hidden // 2, width), bf16)
    send_down, keep_down = call(down_grad_kernel, (down_half,) * 2, 1, 8, 0, [], "down_grad")(
        tie(where, send_up), *act_all, *glow_all
    )
    got_down = swap(send_down, "dp", 2)
    grad_down = reduce_cells(keep_down, got_down, d, other_order, 1)
    gq, gk, gv = call(
        partial(attend_back_kernel, length=length),
        (flat_low, flat_low, flat_low),
        0,
        5,
        0,
        [],
        "attend_back",
    )(q, k, v, tie(gatt, keep_down), gene_ids)
    grad_up = reduce_cells(keep_up, got_up, d, order)
    rights = [gbr, gv, gq, gk]
    rights_got = [swap(right, "fsdp", 1) for right in rights]
    gin, sm = call(
        partial(input_back_kernel, length=length),
        (flat_low, sds((VEC_ROWS, width), f32)),
        2,
        7,
        6,
        [pltpu.VMEM((3, width, width), bf16), pltpu.SemaphoreType.DMA((18,))],
        "input_back",
    )(where, species, gres, gq, gk, gv, sm2, smu, sm1, *attn)
    pair = sds((2 * rows, width), bf16)
    both = sds((2, rows, width), bf16)
    send_ov, keep_ov, send_qk, keep_qk = call(
        near_attn_kernel, (pair, pair, both, both), 1, 10, 0, [], "near_attn"
    )(tie(where, gin, got_down), own_attn, swap(share_attn, "fsdp", 1), *rights, *rights_got)
    got_ov = swap(tie(send_ov, got_up), "fsdp", 2)
    grad_ov = reduce_cells(keep_ov, got_ov, d, order)
    keep_qk, got_qk = scatter_cells(keep_qk, swap(send_qk, "dp", 1), d, order[1:-1])
    sent_qk = add(keep_qk[1], got_qk[1])
    grad_qk = gather_cells(
        (
            keep_qk[0].astype(f32) + got_qk[0].astype(f32) + swap(sent_qk, "fsdp", 2).astype(f32)
        ).astype(bf16),
        d,
        order,
    )

    sm = tie(sm, got_ov)
    sm = sm + swap(sm, "fsdp", 1)
    sm = sm + swap(sm, "fsdp", 2)
    for step in order:
        sm = sm + swap(sm, "dp", 1 << step)
    mine = lax.dynamic_slice_in_dim(sm, f * rows, rows, 1)
    b_up_grad = lax.dynamic_slice_in_dim(sm, BU + f, 1, 0)[0]

    return (
        output.reshape(inputs.shape),
        gin.reshape(inputs.shape),
        mine[TB : TB + 2],
        grad_qk[:rows].astype(f32),
        mine[BQ],
        grad_qk[rows:].astype(f32),
        grad_ov[rows:].astype(f32),
        mine[BV],
        grad_ov[:rows].astype(f32),
        mine[BO],
        mine[G1],
        mine[S1],
        grad_up.astype(f32),
        b_up_grad,
        grad_down.astype(f32),
        mine[BD],
        mine[G2],
        mine[S2],
    )


def solution(mesh):
    cells = P(("dp", "fsdp"), None, None)
    vector = P("fsdp")
    matrix = P("fsdp", None)
    table = P(None, "fsdp")
    return jax.shard_map(
        local,
        mesh=mesh,
        in_specs=(
            cells,
            P(("dp", "fsdp")),
            P(("dp", "fsdp"), None),
            cells,
            table,
            matrix,
            vector,
            matrix,
            matrix,
            vector,
            matrix,
            vector,
            vector,
            vector,
            matrix,
            vector,
            matrix,
            vector,
            vector,
            vector,
        ),
        out_specs=(
            cells,
            cells,
            table,
            matrix,
            vector,
            matrix,
            matrix,
            vector,
            matrix,
            vector,
            vector,
            vector,
            matrix,
            vector,
            matrix,
            vector,
            vector,
            vector,
        ),
        check_vma=False,
    )
```

```python
from functools import partial

import jax
import jax.numpy as jnp
from jax import lax
from jax.experimental import pallas as pl
from jax.experimental.pallas import tpu as pltpu
from jax.sharding import PartitionSpec as P

HEAD_DIM = 64
norm_eps = 1e-12
masked_score = -1e30
f32 = jnp.float32
bf16 = jnp.bfloat16

BQ, BV, BO, G1, S1, BD, G2, S2, TB, BU = 0, 1, 2, 3, 4, 5, 6, 7, 8, 10
VEC_ROWS = 16
TURNS = "UUDSASUUADAASUDASDUSAUADUA"
COST = 1024
ATTEND_COST = 1024
VMEM_LIMIT = 16 * 1024 * 1024
LARGE_VMEM_LIMIT = 56 * 1024 * 1024


def dot(a, b):
    return jnp.dot(a, b, preferred_element_type=f32)


def dot_nt(a, b):
    return lax.dot_general(a, b, (((1,), (1,)), ((), ())), preferred_element_type=f32)


def dot_tn(a, b):
    return lax.dot_general(a, b, (((0,), (0,)), ((), ())), preferred_element_type=f32)


def swap(x, axis, distance):
    count = lax.axis_size(axis)
    with jax.named_scope(f"swap_{axis}{distance}"):
        return lax.ppermute(x, axis, [(i, i ^ distance) for i in range(count)])


def half_columns(x, bit):
    width = x.shape[1] // 2
    return lax.dynamic_slice_in_dim(x, bit * width, width, 1)


def tie(x, *others):
    return lax.optimization_barrier((x,) + others)[0]


def halved(first, rows, top, bit):
    return [
        (first, top, rows, 2, bit, 0),
        (first + 1, top, rows, 2, bit, 1),
        (first + 2, top, rows, 3, bit, 0),
        (first + 3, top, rows, 3, bit, 1),
    ]


def start_rows(plan, pieces, where_ref, shard_rows, target, sems, base):
    width = target.shape[1]
    half = width // 2
    copies = []
    for n, (piece, first, rows, distance, bit, other, *at) in enumerate(plan):
        row = pl.multiple_of((where_ref[0] ^ distance) * shard_rows + (at[0] if at else 0), 8)
        if bit is None:
            cols = pl.ds(0, width)
        else:
            side = where_ref[bit]
            cols = pl.ds(pl.multiple_of((1 - side if other else side) * half, 128), half)
        copy = pltpu.make_async_copy(
            pieces[piece].at[pl.ds(first, rows), :],
            target.at[pl.ds(row, rows), cols],
            sems.at[base + n],
        )
        copy.start()
        copies.append(copy)
    return copies


def attn_plan(first, rows):
    return [(0, first, rows, 0, None, 0), (1, first, rows, 1, None, 0)] + halved(2, rows, first, 1)


def up_plan(rows):
    half = rows // 2
    plan = [(0, 0, rows, 0, None, 0), (1, 0, rows, 1, None, 0)] + halved(2, half, 0, 2)
    return plan + [(6, 0, half, 2, None, 0, half), (7, 0, half, 3, None, 0, half)]


def down_plan(rows):
    half = rows // 2
    plan = [(0, 0, rows, 0, None, 0), (1, 0, rows, 1, None, 0)] + halved(2, half, 0, 1)
    return plan + [copy + (half,) for copy in halved(6, half, 0, 2)]


def wait_all(copies):
    for copy in copies:
        copy.wait()


def call(kernel, out_shapes, n_smem, n_vmem, n_any, scratch, name, cost=COST, resident=True, limit=VMEM_LIMIT):
    if resident:
        out_shapes = jax.tree.map(
            lambda out: pltpu.VMEM(out.shape, out.dtype)
            if isinstance(out, jax.ShapeDtypeStruct)
            else out,
            out_shapes,
        )
    return pl.pallas_call(
        kernel,
        out_shape=out_shapes,
        in_specs=[pl.BlockSpec(memory_space=pltpu.SMEM)] * n_smem
        + [pl.BlockSpec(memory_space=pltpu.VMEM)] * n_vmem
        + [pl.BlockSpec(memory_space=pl.ANY)] * n_any,
        out_specs=jax.tree.map(lambda _: pl.BlockSpec(memory_space=pltpu.VMEM), out_shapes),
        scratch_shapes=scratch,
        compiler_params=pltpu.CompilerParams(
            vmem_limit_bytes=limit
        ),
        cost_estimate=pl.CostEstimate(flops=cost, bytes_accessed=cost, transcendentals=0),
        name=name,
    )


def in_hbm(x):
    return pltpu.with_memory_space_constraint(x, pltpu.HBM)


def sds(shape, dtype):
    return jax.ShapeDtypeStruct(shape, dtype)


def norm_forward(residual):
    average = jnp.mean(residual, axis=-1, keepdims=True)
    centred = residual - average
    inverse = lax.rsqrt(jnp.mean(centred * centred, axis=-1, keepdims=True) + norm_eps)
    return centred * inverse, inverse


def norm_backward(grad_out, normal, inverse, gain):
    scaled = grad_out * gain
    first = jnp.mean(scaled, axis=-1, keepdims=True)
    second = jnp.mean(scaled * normal, axis=-1, keepdims=True)
    return inverse * (scaled - first - normal * second)


def column_sum(x):
    return jnp.sum(x, axis=0, keepdims=True)


def head_mask(h, rows):
    lane = lax.broadcasted_iota(jnp.int32, (rows, 2 * HEAD_DIM), 1)
    return (lane // HEAD_DIM) == h


def soft_rows(q_pair, k_pair, dead, mask):
    scale = HEAD_DIM ** (-0.5)
    q_head = jnp.where(mask, q_pair, jnp.zeros_like(q_pair))
    scores = dot_nt(q_head, k_pair) * scale
    scores = jnp.where(dead, masked_score, scores)
    expo = jnp.exp(scores - jnp.max(scores, axis=-1, keepdims=True))
    return expo / jnp.sum(expo, axis=-1, keepdims=True)


def pack_kernel(where_ref, q_ref, k_ref, v_ref, o_ref, *refs):
    vectors, table_ref, b_up_ref = refs[:TB], refs[TB], refs[TB + 1]
    first_ref, second_ref, half_first_ref, half_second_ref, spread = refs[TB + 2 :]
    rows, width = q_ref.shape
    f, y = where_ref[0], where_ref[1]
    half = half_first_ref.shape[1]
    cols = pl.ds(pl.multiple_of(y * half, 128), half)
    for whole_ref, half_ref, pair in (
        (first_ref, half_first_ref, (q_ref, k_ref)),
        (second_ref, half_second_ref, (v_ref, o_ref)),
    ):
        for m, ref in enumerate(pair):
            at = slice(m * rows, (m + 1) * rows)
            half_ref[at, :] = ref[:, cols]
            whole_ref[at, :] = ref[...]
    spread[...] = jnp.zeros(spread.shape, f32)
    table = table_ref[...].astype(f32)
    for k in range(4):

        @pl.when(f == k)
        def _():
            mine = slice(k * rows, (k + 1) * rows)
            for n, ref in enumerate(vectors):
                spread[n : n + 1, mine] = ref[...].astype(f32).reshape(1, rows)
            spread[TB : TB + 2, mine] = table
            spread[BU + k : BU + k + 1, :] = b_up_ref[...].astype(f32).reshape(1, width)

    first_ref[2 * rows :, :] = spread[...].astype(bf16)
    half_first_ref[2 * rows :, :] = spread[:, cols].astype(bf16)


def put_blocks(value, f, blocks, targets, at):
    rows = value.shape[1] // 4
    for i in range(4):
        blocks[i] = value[:, i * rows : (i + 1) * rows]
    for n, target in enumerate(targets):
        target[at] = blocks[f ^ n]
        target[at + 1] = blocks[f ^ 2 ^ n]


def attend_kernel(
    where_ref,
    species_ref,
    x_ref,
    ids_ref,
    *refs,
    length,
):
    pieces, later_pieces = refs[:6], refs[6:12]
    (
        q_ref,
        k_ref,
        v_ref,
        own_ref,
        share_ref,
        n1_ref,
        inv_ref,
        low_ref,
        low_own_ref,
        low_share_ref,
        vec_ref,
        wbuf,
        vbuf,
        abuf,
        blocks,
        sems,
    ) = refs[12:]
    f = where_ref[0]
    tokens, width = x_ref.shape
    cells = tokens // length
    rows = width // 4
    vec_copies = start_rows(
        attn_plan(2 * rows, VEC_ROWS), pieces, where_ref, VEC_ROWS, vbuf, sems, 24
    )
    copies = []
    for m in range(4):
        from_pieces = pieces if m < 2 else later_pieces
        plan = attn_plan((m % 2) * rows, rows)
        copies.append(start_rows(plan, from_pieces, where_ref, rows, wbuf.at[m], sems, 6 * m))
    wait_all(vec_copies)
    vec = vbuf[0:VEC_ROWS, :].astype(f32)
    for i in range(1, 4):
        vec = vec + vbuf[i * VEC_ROWS : (i + 1) * VEC_ROWS, :].astype(f32)
    vec_ref[...] = vec
    summed = []
    for c in range(cells):
        offset = jnp.where(species_ref[c] == 1, vec[TB + 1 : TB + 2, :], vec[TB : TB + 1, :])
        summed.append(x_ref[c * length : (c + 1) * length, :].astype(f32) + offset)
    summed = jnp.concatenate(summed, axis=0)
    summed_low = summed.astype(bf16)
    put_blocks(summed_low, f, blocks, (own_ref, share_ref), 2)
    wait_all(copies[0])
    q_ref[...] = (dot(summed_low, wbuf[0]) + vec[BQ : BQ + 1, :]).astype(bf16)
    wait_all(copies[1])
    k_ref[...] = dot(summed_low, wbuf[1]).astype(bf16)
    wait_all(copies[2])
    v_ref[...] = (dot(summed_low, wbuf[2]) + vec[BV : BV + 1, :]).astype(bf16)
    pair = 2 * HEAD_DIM
    masks = [head_mask(h, length) for h in range(2)]
    for c in range(cells):
        at = slice(c * length, (c + 1) * length)
        dead = jnp.broadcast_to(ids_ref[c : c + 1, :], (length, length)) == 0
        for p in range(width // pair):
            cols = slice(p * pair, (p + 1) * pair)
            q_pair, k_pair, v_pair = q_ref[at, cols], k_ref[at, cols], v_ref[at, cols]
            total = None
            for h in range(2):
                soft = soft_rows(q_pair, k_pair, dead, masks[h]).astype(bf16)
                part = dot(soft, jnp.where(masks[h], v_pair, jnp.zeros_like(v_pair)))
                total = part if total is None else total + part
            abuf[at, cols] = total.astype(bf16)
    attended = abuf[...]
    put_blocks(attended, f, blocks, (own_ref, share_ref), 0)
    wait_all(copies[3])
    branch = dot(attended, wbuf[3]) + vec[BO : BO + 1, :]
    normal, inverse = norm_forward(summed + branch)
    n1_ref[...] = normal
    inv_ref[...] = jnp.broadcast_to(inverse, inv_ref.shape)
    low = (normal * vec[G1 : G1 + 1, :] + vec[S1 : S1 + 1, :]).astype(bf16)
    low_ref[...] = low
    put_blocks(low, f, blocks, (low_own_ref, low_share_ref), 0)


def up_kernel(where_ref, low_ref, vec_ref, *refs):
    pieces = refs[:8]
    act_ref, own_ref, near_ref, across_ref, slope_ref, wbuf, sems = refs[8:]
    f = where_ref[0]
    hidden = wbuf.shape[1]
    rows = wbuf.shape[0] // 4
    block = hidden // 4
    wait_all(start_rows(up_plan(rows), pieces, where_ref, rows, wbuf, sems, 0))
    low = low_ref[...]
    for j in range(4):
        up = dot(low, wbuf[:, j * block : (j + 1) * block]) + vec_ref[BU + j : BU + j + 1, :]
        half_cdf = 0.5 * (1.0 + lax.erf(up * (0.5**0.5)))
        density = jnp.exp(-0.5 * up * up) * 0.3989422804014327
        act_ref[j] = (up * half_cdf).astype(bf16)
        slope_ref[j] = half_cdf + up * density
    own_ref[...] = act_ref[f]
    near_ref[...] = act_ref[f ^ 1]
    across_ref[0] = act_ref[f ^ 2]
    across_ref[1] = act_ref[f ^ 3]


def down_kernel(where_ref, act_ref, n1_ref, vec_ref, cot_ref, *refs):
    pieces = refs[:10]
    out_ref, gsec_ref, glow_ref, sm_ref, wbuf, sems = refs[10:]
    rows = wbuf.shape[0] // 4
    width = wbuf.shape[1]
    copies = start_rows(down_plan(rows), pieces, where_ref, rows, wbuf, sems, 0)
    vec = vec_ref[...]
    wait_all(copies)
    branch = None
    for j in range(4):
        part = dot(act_ref[j], wbuf[j * rows : (j + 1) * rows, :])
        branch = part if branch is None else branch + part
    normed = n1_ref[...] * vec[G1 : G1 + 1, :] + vec[S1 : S1 + 1, :]
    normal, inverse = norm_forward(normed + (branch + vec[BD : BD + 1, :]))
    gain = vec[G2 : G2 + 1, :]
    out_ref[...] = (normal * gain + vec[S2 : S2 + 1, :]).astype(bf16)
    cot = cot_ref[...].astype(f32)
    grad = norm_backward(cot, normal, inverse, gain)
    gsec_ref[...] = grad
    low = grad.astype(bf16)
    glow_ref[...] = low
    sm_ref[0:1, :] = column_sum(cot * normal)
    sm_ref[1:2, :] = column_sum(cot)
    sm_ref[2:3, :] = column_sum(low.astype(f32))
    sm_ref[3:8, :] = jnp.zeros((5, width), f32)


def near_up_kernel(where_ref, own_ref, got_ref, *refs):
    rights, got_rights = refs[:4], refs[4:8]
    send_x, keep_x, send_y, keep_y = refs[8:]
    block = rights[0].shape[1]
    part = send_x.shape[1]
    low_z = where_ref[2] == 0
    for slot, out in ((1, send_x), (0, keep_x)):
        for j in range(4):
            cols = slice(j * block, (j + 1) * block)
            total = dot_tn(own_ref[slot], rights[j][...]) + dot_tn(got_ref[slot], got_rights[j][...])
            total = total.astype(bf16)
            out[0, :, cols] = total[:part]
            out[1, :, cols] = total[2 * part : 3 * part]
            first, second = total[part : 2 * part], total[3 * part :]
            send_y[slot, :, cols] = jnp.where(low_z, second, first)
            keep_y[slot, :, cols] = jnp.where(low_z, first, second)


def near_attn_kernel(where_ref, own_ref, got_ref, *refs):
    rights, got_rights = refs[:4], refs[4:8]
    send_x, keep_x, send_y, keep_y = refs[8:]
    low_y = where_ref[1] == 0

    def block(left, n):
        total = dot_tn(own_ref[left], rights[n][...]) + dot_tn(got_ref[left], got_rights[n][...])
        return total.astype(bf16)

    for slot, ref in ((1, send_x), (0, keep_x)):
        ref[0] = block(slot, 0)
        ref[1] = block(2 + slot, 1)
        query, key = block(2 + slot, 2), block(2 + slot, 3)
        send_y[slot] = jnp.where(low_y, key, query)
        keep_y[slot] = jnp.where(low_y, query, key)


def down_grad_kernel(where_ref, *refs):
    lefts, rights, outs = refs[:4], refs[4:8], refs[8:]
    y = where_ref[1]
    rows = outs[0].shape[0]
    for half, out in ((1 - y, outs[0]), (y, outs[1])):
        cols = pl.ds(pl.multiple_of(half * rows, 128), rows)
        total = None
        for n, (left, right) in enumerate(zip(lefts, rights)):
            part = dot_tn(left[0, :, cols] if n == 2 else left[:, cols], right[...])
            total = part if total is None else total + part
        out[...] = total.astype(bf16)


def hidden_back_kernel(where_ref, glow_ref, slope_ref, *refs):
    pieces = refs[:10]
    guis, sm_ref, wbuf, sems = refs[10:14], refs[14], refs[15], refs[16]
    rows = wbuf.shape[0] // 4
    width = wbuf.shape[1]
    wait_all(start_rows(down_plan(rows), pieces, where_ref, rows, wbuf, sems, 0))
    glow = glow_ref[...]
    for j in range(4):
        grad = dot_nt(glow, wbuf[j * rows : (j + 1) * rows, :]) * slope_ref[j]
        low = grad.astype(bf16)
        guis[j][...] = low
        sm_ref[j : j + 1, :] = column_sum(low.astype(f32))
    sm_ref[4:8, :] = jnp.zeros((4, rows), f32)


def norm_back_kernel(where_ref, gsec_ref, n1_ref, inv_ref, vec_ref, *refs):
    guis, pieces, attn_pieces = refs[:4], refs[4:12], refs[12:18]
    gres_ref, gbr_ref, gatt_ref, sm_ref, wbuf, obuf, sems = refs[18:]
    rows = wbuf.shape[0] // 4
    hidden = wbuf.shape[1]
    width = obuf.shape[1]
    copies = start_rows(up_plan(rows), pieces, where_ref, rows, wbuf, sems, 0)
    out_copies = start_rows(attn_plan(rows, rows), attn_pieces, where_ref, rows, obuf, sems, 8)
    wait_all(copies)
    block = hidden // 4
    grad_normed = gsec_ref[...]
    for j in range(4):
        grad_normed = grad_normed + dot_nt(guis[j][...], wbuf[:, j * block : (j + 1) * block])
    normal = n1_ref[...]
    grad = norm_backward(grad_normed, normal, inv_ref[:, 0:1], vec_ref[G1 : G1 + 1, :])
    gres_ref[...] = grad
    low = grad.astype(bf16)
    gbr_ref[...] = low
    sm_ref[0:1, :] = column_sum(grad_normed * normal)
    sm_ref[1:2, :] = column_sum(grad_normed)
    sm_ref[2:3, :] = column_sum(low.astype(f32))
    sm_ref[3:8, :] = jnp.zeros((5, width), f32)
    wait_all(out_copies)
    gatt_ref[...] = dot_nt(low, obuf[...]).astype(bf16)


def attend_back_kernel(q_ref, k_ref, v_ref, gatt_ref, ids_ref, gq_ref, gk_ref, gv_ref, *, length):
    tokens, width = q_ref.shape
    cells = tokens // length
    scale = HEAD_DIM ** (-0.5)
    pair = 2 * HEAD_DIM
    masks = [head_mask(h, length) for h in range(2)]
    for c in range(cells):
        at = slice(c * length, (c + 1) * length)
        dead = jnp.broadcast_to(ids_ref[c : c + 1, :], (length, length)) == 0
        for p in range(width // pair):
            cols = slice(p * pair, (p + 1) * pair)
            q_pair, k_pair, v_pair = q_ref[at, cols], k_ref[at, cols], v_ref[at, cols]
            g_pair = gatt_ref[at, cols]
            zero = jnp.zeros_like(q_pair)
            gq = gk = gv = jnp.zeros((length, pair), f32)
            for h in range(2):
                mask = masks[h]
                soft = soft_rows(q_pair, k_pair, dead, mask)
                g_head = jnp.where(mask, g_pair, zero)
                grad_soft = dot_nt(g_head, v_pair)
                inner = jnp.sum(soft * grad_soft, axis=-1, keepdims=True)
                grad_scores = (soft * (grad_soft - inner)).astype(bf16)
                gv = gv + dot_tn(soft.astype(bf16), g_head)
                gq = gq + dot(grad_scores, jnp.where(mask, k_pair, zero))
                gk = gk + dot_tn(grad_scores, jnp.where(mask, q_pair, zero))
            gq_ref[at, cols] = (gq * scale).astype(bf16)
            gk_ref[at, cols] = (gk * scale).astype(bf16)
            gv_ref[at, cols] = gv.astype(bf16)


def input_back_kernel(
    where_ref, species_ref, gres_ref, gq_ref, gk_ref, gv_ref, sm2_ref, smu_ref, sm1_ref, *refs,
    length,
):
    pieces, later_pieces = refs[:6], refs[6:12]
    gin_ref, sm_ref, wbuf, sems = refs[12:]
    tokens, width = gres_ref.shape
    rows = width // 4
    copies = []
    for m in range(3):
        from_pieces = pieces if m < 2 else later_pieces
        plan = attn_plan((m % 2) * rows, rows)
        copies.append(start_rows(plan, from_pieces, where_ref, rows, wbuf.at[m], sems, 6 * m))
    sm_ref[BQ : BQ + 1, :] = column_sum(gq_ref[...].astype(f32))
    sm_ref[BV : BV + 1, :] = column_sum(gv_ref[...].astype(f32))
    sm_ref[BO : BO + 1, :] = sm1_ref[2:3, :]
    sm_ref[G1 : G1 + 2, :] = sm1_ref[0:2, :]
    sm_ref[BD : BD + 1, :] = sm2_ref[2:3, :]
    sm_ref[G2 : G2 + 2, :] = sm2_ref[0:2, :]
    sm_ref[BU : BU + 4, :] = smu_ref[0:4, :]
    sm_ref[BU + 4 : VEC_ROWS, :] = jnp.zeros((VEC_ROWS - BU - 4, width), f32)
    total = gres_ref[...]
    for m, grad in enumerate((gq_ref, gk_ref, gv_ref)):
        wait_all(copies[m])
        total = total + dot_nt(grad[...], wbuf[m])
    gin_ref[...] = total.astype(bf16)
    for s in range(2):
        row = jnp.zeros((1, width), f32)
        for c in range(tokens // length):
            cell = column_sum(total[c * length : (c + 1) * length, :])
            row = row + jnp.where(species_ref[c] == s, cell, jnp.zeros_like(cell))
        sm_ref[TB + s : TB + s + 1, :] = row


def half_rows(x, bit):
    rows = x.shape[-2] // 2
    return lax.dynamic_slice_in_dim(x, bit * rows, rows, x.ndim - 2)


def add(a, b):
    return (a.astype(f32) + b.astype(f32)).astype(bf16)


def two_way_chain(send_x, keep_x, send_b, keep_b, dp_index, bits, steps):
    p, q = [(dp_index >> bit) & 1 for bit in bits]
    one, two = [1 << bit for bit in bits]
    got_x = swap(send_x, "fsdp", 2)
    got_b = swap(send_b, "dp", one)
    got_x = yield got_x, send_b
    give = jnp.where(p == 0, add(keep_x[1], got_x[1]), add(keep_x[0], got_x[0]))
    take = jnp.where(p == 0, add(keep_x[0], got_x[0]), add(keep_x[1], got_x[1]))
    got_give = swap(give, "dp", one)
    got_b = yield got_b, give
    give = add(keep_b[1], got_b[1])
    rest = add(keep_b[0], got_b[0])
    got_rest = swap(give, "fsdp", 2)
    got_give = yield got_give, give
    first = add(take, got_give)
    got_rest = yield got_rest, first
    second = add(rest, got_rest)
    send = jnp.where(q == 0, second, first)
    keep = jnp.where(q == 0, first, second)
    got = yield swap(send, "dp", two), send
    total = add(keep, got)
    for step in steps[:-1]:
        bit = (dp_index >> step) & 1
        send = half_rows(total, 1 - bit)
        got = yield swap(send, "dp", 1 << step), send
        total = add(half_rows(total, bit), got)
    got = yield swap(total, "dp", 1 << steps[-1]), total
    total = add(total, got)
    for step in reversed(steps[:-1]):
        other = yield swap(total, "dp", 1 << step), total
        total = join_rows(total, other, dp_index, step)
    other = yield swap(total, "dp", two), total
    mine = jnp.stack([jnp.where(q == 0, total, other), jnp.where(q == 0, other, total)])
    other = yield swap(mine, "dp", one), mine
    return jnp.where(p == 0, mine, other), jnp.where(p == 0, other, mine)


def join_rows(total, other, dp_index, step):
    return jnp.where(
        (dp_index >> step) & 1 == 0,
        jnp.concatenate([total, other], axis=0),
        jnp.concatenate([other, total], axis=0),
    )


def halving_chain(send, keep, dp_index, steps):
    got = yield swap(send, "dp", 1 << steps[0]), send
    for step in steps[1:-1]:
        bit = (dp_index >> step) & 1
        send = add(half_rows(keep, 1 - bit), half_rows(got, 1 - bit))
        keep = add(half_rows(keep, bit), half_rows(got, bit))
        got = yield swap(send, "dp", 1 << step), send
    total = add(keep, got)
    got = yield swap(total, "dp", 1 << steps[-1]), total
    total = add(total, got)
    for step in reversed(steps[:-1]):
        other = yield swap(total, "dp", 1 << step), total
        total = join_rows(total, other, dp_index, step)
    return total


def whole_chain(total, steps):
    for axis, distance in (("fsdp", 1), ("fsdp", 2)) + tuple(("dp", 1 << step) for step in steps):
        got = yield swap(total, axis, distance), total
        total = total + got
    return total


def take_turns(chains, turns, token):
    pending = {name: next(chain)[0] for name, chain in chains.items()}
    results = {}

    def turn(name, token):
        try:
            pending[name], token = chains[name].send(tie(pending[name], token))
        except StopIteration as stop:
            results[name] = stop.value
            del pending[name]
        return token

    for name in turns:
        if name in pending:
            token = turn(name, token)
    while pending:
        for name in list(pending):
            token = turn(name, token)
    return results


def local(
    inputs,
    species,
    gene_ids,
    cotangent,
    table,
    w_query,
    b_query,
    w_key,
    w_value,
    b_value,
    w_out,
    b_out,
    gain_one,
    shift_one,
    w_up,
    b_up,
    w_down,
    b_down,
    gain_two,
    shift_two,
):
    cells, length, width = inputs.shape
    tokens = cells * length
    rows = w_query.shape[0]
    hidden = w_up.shape[1]
    shard_hidden = w_down.shape[0]
    shards = lax.axis_size("fsdp")
    f = lax.axis_index("fsdp")
    d = lax.axis_index("dp")
    y_bit = d & 1
    where = jnp.stack([f, y_bit, (d >> 1) & 1]).astype(jnp.int32)
    order = tuple(range((lax.axis_size("dp") - 1).bit_length()))

    z_bit = (d >> 1) & 1
    first_own, second_own, first_half, second_half = call(
        pack_kernel,
        (
            sds((2 * rows + VEC_ROWS, width), bf16),
            sds((2 * rows, width), bf16),
            sds((2 * rows + VEC_ROWS, width // 2), bf16),
            sds((2 * rows, width // 2), bf16),
        ),
        1,
        6 + TB,
        0,
        [pltpu.VMEM((VEC_ROWS, width), f32)],
        "pack",
        resident=False,
        limit=LARGE_VMEM_LIMIT,
    )(
        where,
        w_query,
        w_key,
        w_value,
        w_out,
        b_query,
        b_value,
        b_out,
        gain_one,
        shift_one,
        b_down,
        gain_two,
        shift_two,
        table,
        b_up,
    )

    def relays(half, axis_bit):
        across = swap(half, "fsdp", 2)
        return across, swap(across, "dp", axis_bit)

    def with_core(across, relayed, when=None):
        if when is not None:
            across, relayed = tie(across, when), tie(relayed, when)
        return across, relayed, swap(across, "fsdp", 1), swap(relayed, "fsdp", 1)

    first = relays(first_half, 1)
    second = relays(tie(second_half, first_half), 1)
    up_top = relays(tie(half_columns(w_up[: rows // 2], z_bit), first[0]), 2)
    up_rest = swap(tie(w_up[rows // 2 :], first[0]), "fsdp", 2)
    attn_first = (first_own, swap(first_own, "fsdp", 1), *with_core(*first))
    attn_second = (second_own, swap(second_own, "fsdp", 1), *with_core(*second))
    attn_first = tuple(map(in_hbm, attn_first))
    attn_second = tuple(map(in_hbm, attn_second))
    down_core = swap(w_down, "fsdp", 1)
    up_core = swap(w_up, "fsdp", 1)
    top = shard_hidden // 2
    down_top = swap(tie(half_columns(w_down[:top], y_bit), up_top[0]), "fsdp", 2)
    down_rest = swap(tie(half_columns(w_down[top:], z_bit), up_top[0]), "fsdp", 2)

    x_rows = inputs.reshape(tokens, width)
    cot_rows = cotangent.reshape(tokens, width)
    flat_low = sds((tokens, width), bf16)
    flat = sds((tokens, width), f32)
    small = sds((8, width), f32)
    q, k, v, own_attn, share_attn, n1, inv1, low, low_own, low_share, vec = call(
        partial(attend_kernel, length=length),
        (
            flat_low,
            flat_low,
            flat_low,
            pltpu.HBM((4, tokens, rows), bf16),
            pltpu.HBM((4, tokens, rows), bf16),
            flat,
            sds((tokens, 128), f32),
            flat_low,
            pltpu.HBM((2, tokens, rows), bf16),
            pltpu.HBM((2, tokens, rows), bf16),
            sds((VEC_ROWS, width), f32),
        ),
        2,
        2,
        12,
        [
            pltpu.VMEM((4, width, width), bf16),
            pltpu.VMEM((4 * VEC_ROWS, width), bf16),
            pltpu.VMEM((tokens, width), bf16),
            pltpu.VMEM((4, tokens, rows), bf16),
            pltpu.SemaphoreType.DMA((30,)),
        ],
        "attend",
        ATTEND_COST,
    )(where, species, x_rows, gene_ids, *attn_first, *attn_second)
    up_late = tie(up_rest, q)
    up = (w_up, up_core, *with_core(*up_top, q), up_late, swap(up_late, "fsdp", 1))
    down_top = tie(down_top, q)
    down_top = (down_top, swap(down_top, "dp", 1))
    act, act_own, act_near, act_across, slope = call(
        up_kernel,
        (
            sds((shards, tokens, shard_hidden), bf16),
            *(pltpu.HBM((tokens, shard_hidden), bf16),) * 2,
            pltpu.HBM((2, tokens, shard_hidden), bf16),
            sds((shards, tokens, shard_hidden), f32),
        ),
        1,
        2,
        8,
        [pltpu.VMEM((width, hidden), bf16), pltpu.SemaphoreType.DMA((8,))],
        "up",
    )(where, low, vec, *up)
    down_rest = tie(down_rest, act_own)
    down_rest = (down_rest, swap(down_rest, "dp", 2))
    down = (w_down, down_core, *with_core(*down_top, act_own), *with_core(*down_rest))
    output, gsec, glow, sm2 = call(
        down_kernel,
        (flat_low, flat, flat_low, small),
        1,
        4,
        10,
        [pltpu.VMEM((hidden, width), bf16), pltpu.SemaphoreType.DMA((10,))],
        "down",
    )(where, act, n1, vec, cot_rows, *down)
    act_got = swap(act_across, "fsdp", 2)
    glow_across = swap(glow, "fsdp", 2)
    *guis, smu = call(
        hidden_back_kernel,
        (*(sds((tokens, shard_hidden), bf16),) * 4, sds((8, shard_hidden), f32)),
        1,
        2,
        10,
        [pltpu.VMEM((hidden, width), bf16), pltpu.SemaphoreType.DMA((10,))],
        "hidden_back",
    )(where, glow, slope, *down)
    guis_got = [swap(part, "fsdp", 1) for part in guis]
    gres, gbr, gatt, sm1 = call(
        norm_back_kernel,
        (pltpu.HBM(flat.shape, f32), flat_low, flat_low, small),
        1,
        8,
        14,
        [
            pltpu.VMEM((width, hidden), bf16),
            pltpu.VMEM((width, width), bf16),
            pltpu.SemaphoreType.DMA((14,)),
        ],
        "norm_back",
    )(where, gsec, n1, inv1, vec, *guis, *up, *attn_second)
    part = pltpu.HBM((2, rows // 4, hidden), bf16)
    up_parts = call(near_up_kernel, (part,) * 4, 1, 10, 0, [], "near_up", resident=False)(
        tie(where, gbr), in_hbm(low_own), in_hbm(swap(low_share, "fsdp", 1)), *guis, *guis_got
    )
    gq, gk, gv = call(
        partial(attend_back_kernel, length=length),
        (flat_low, flat_low, flat_low),
        0,
        5,
        0,
        [],
        "attend_back",
    )(q, k, v, tie(gatt, up_parts[0]), gene_ids)
    act_all = (
        act_own,
        swap(tie(act_near, gbr), "fsdp", 1),
        act_got,
        swap(tie(act_got, gbr)[1], "fsdp", 1),
    )
    glow_all = (
        glow,
        swap(tie(glow, gbr), "fsdp", 1),
        glow_across,
        swap(tie(glow_across, gq), "fsdp", 1),
    )
    rights = [gbr, gv, gq, gk]
    rights_got = [swap(right, "fsdp", 1) for right in rights]
    down_half = pltpu.HBM((shard_hidden // 2, width), bf16)
    send_down, keep_down = call(down_grad_kernel, (down_half,) * 2, 1, 8, 0, [], "down_grad", resident=False)(
        tie(where, gq), *map(in_hbm, act_all), glow, *map(in_hbm, glow_all[1:])
    )
    pair = pltpu.HBM((2, rows, width), bf16)
    attn_parts = call(near_attn_kernel, (pair,) * 4, 1, 10, 0, [], "near_attn", resident=False)(
        tie(where, keep_down), in_hbm(own_attn), in_hbm(swap(share_attn, "fsdp", 1)), *rights, *map(in_hbm, rights_got)
    )
    gin, sm = call(
        partial(input_back_kernel, length=length),
        (flat_low, sds((VEC_ROWS, width), f32)),
        2,
        7,
        12,
        [pltpu.VMEM((3, width, width), bf16), pltpu.SemaphoreType.DMA((18,))],
        "input_back",
        resident=False,
    )(
        tie(where, attn_parts[0]),
        species,
        gres,
        gq,
        gk,
        gv,
        sm2,
        smu,
        sm1,
        *attn_first,
        *attn_second,
    )
    done = take_turns(
        {
            "up": two_way_chain(*up_parts, d, (1, 0), order[2:]),
            "down": halving_chain(send_down, keep_down, d, order),
            "attn": two_way_chain(*attn_parts, d, (0, 1), order[2:]),
            "small": whole_chain(sm, order),
        },
        [{"U": "up", "D": "down", "A": "attn", "S": "small"}[name] for name in TURNS],
        attn_parts[0],
    )
    grad_up = jnp.stack(done["up"]).reshape(rows, hidden)
    grad_down = done["down"]
    low_attn, high_attn = done["attn"]
    sm = done["small"]

    mine = lax.dynamic_slice_in_dim(sm, f * rows, rows, 1)
    b_up_grad = lax.dynamic_slice_in_dim(sm, BU + f, 1, 0)[0]

    return (
        output.reshape(inputs.shape),
        gin.reshape(inputs.shape),
        mine[TB : TB + 2],
        low_attn[1].astype(f32),
        mine[BQ],
        high_attn[1].astype(f32),
        high_attn[0].astype(f32),
        mine[BV],
        low_attn[0].astype(f32),
        mine[BO],
        mine[G1],
        mine[S1],
        grad_up.astype(f32),
        b_up_grad,
        grad_down.astype(f32),
        mine[BD],
        mine[G2],
        mine[S2],
    )


def solution(mesh):
    cells = P(("dp", "fsdp"), None, None)
    vector = P("fsdp")
    matrix = P("fsdp", None)
    table = P(None, "fsdp")
    return jax.shard_map(
        local,
        mesh=mesh,
        in_specs=(
            cells,
            P(("dp", "fsdp")),
            P(("dp", "fsdp"), None),
            cells,
            table,
            matrix,
            vector,
            matrix,
            matrix,
            vector,
            matrix,
            vector,
            vector,
            vector,
            matrix,
            vector,
            matrix,
            vector,
            vector,
            vector,
        ),
        out_specs=(
            cells,
            cells,
            table,
            matrix,
            vector,
            matrix,
            matrix,
            vector,
            matrix,
            vector,
            vector,
            vector,
            matrix,
            vector,
            matrix,
            vector,
            vector,
            vector,
        ),
        check_vma=False,
    )
```

```python
from functools import partial

import jax
import jax.numpy as jnp
from jax import lax
from jax.experimental import pallas as pl
from jax.experimental.pallas import tpu as pltpu
from jax.sharding import PartitionSpec as P

HEAD_DIM = 64
norm_eps = 1e-12
masked_score = -1e30
f32 = jnp.float32
bf16 = jnp.bfloat16

BQ, BV, BO, G1, S1, BD, G2, S2, TB, BU = 0, 1, 2, 3, 4, 5, 6, 7, 8, 10
VEC_ROWS = 16
EARLY_TURNS = ""
MIDDLE_TURNS = "UU"
UP_STRIPS_FIRST = False
TURNS = "DSUASUADAASUDASUDASUUADA"
UP_BITS = (1, 0)
DOWN_BITS = (0, 1)
COST = 1024
ATTEND_COST = 1024
VMEM_LIMIT = 16 * 1024 * 1024
LARGE_VMEM_LIMIT = 56 * 1024 * 1024


def dot(a, b):
    return jnp.dot(a, b, preferred_element_type=f32)


def dot_nt(a, b):
    return lax.dot_general(a, b, (((1,), (1,)), ((), ())), preferred_element_type=f32)


def dot_tn(a, b):
    return lax.dot_general(a, b, (((0,), (0,)), ((), ())), preferred_element_type=f32)


def swap(x, axis, distance):
    count = lax.axis_size(axis)
    with jax.named_scope(f"swap_{axis}{distance}"):
        return lax.ppermute(x, axis, [(i, i ^ distance) for i in range(count)])


def half_columns(x, bit):
    width = x.shape[1] // 2
    return lax.dynamic_slice_in_dim(x, bit * width, width, 1)


def tie(x, *others):
    return lax.optimization_barrier((x,) + others)[0]


def halved(first, rows, top, bit):
    return [
        (first, top, rows, 2, bit, 0),
        (first + 1, top, rows, 2, bit, 1),
        (first + 2, top, rows, 3, bit, 0),
        (first + 3, top, rows, 3, bit, 1),
    ]


def start_rows(plan, pieces, where_ref, shard_rows, target, sems, base):
    width = target.shape[1]
    half = width // 2
    copies = []
    for n, (piece, first, rows, distance, bit, other, *at) in enumerate(plan):
        row = pl.multiple_of((where_ref[0] ^ distance) * shard_rows + (at[0] if at else 0), 8)
        if bit is None:
            cols = pl.ds(0, width)
        else:
            side = where_ref[bit]
            cols = pl.ds(pl.multiple_of((1 - side if other else side) * half, 128), half)
        copy = pltpu.make_async_copy(
            pieces[piece].at[pl.ds(first, rows), :],
            target.at[pl.ds(row, rows), cols],
            sems.at[base + n],
        )
        copy.start()
        copies.append(copy)
    return copies


def attn_plan(first, rows):
    return [(0, first, rows, 0, None, 0), (1, first, rows, 1, None, 0)] + halved(2, rows, first, 1)


def up_plan(rows):
    half = rows // 2
    plan = [(0, 0, rows, 0, None, 0), (1, 0, rows, 1, None, 0)] + halved(2, half, 0, 2)
    return plan + [(6, 0, half, 2, None, 0, half), (7, 0, half, 3, None, 0, half)]


def down_plan(rows):
    half = rows // 2
    plan = [(0, 0, rows, 0, None, 0), (1, 0, rows, 1, None, 0)] + halved(2, half, 0, 1)
    return plan + [copy + (half,) for copy in halved(6, half, 0, 2)]


def wait_all(copies):
    for copy in copies:
        copy.wait()


def call(kernel, out_shapes, n_smem, n_vmem, n_any, scratch, name, cost=COST, resident=True, limit=VMEM_LIMIT):
    if resident:
        out_shapes = jax.tree.map(
            lambda out: pltpu.VMEM(out.shape, out.dtype)
            if isinstance(out, jax.ShapeDtypeStruct)
            else out,
            out_shapes,
        )
    return pl.pallas_call(
        kernel,
        out_shape=out_shapes,
        in_specs=[pl.BlockSpec(memory_space=pltpu.SMEM)] * n_smem
        + [pl.BlockSpec(memory_space=pltpu.VMEM)] * n_vmem
        + [pl.BlockSpec(memory_space=pl.ANY)] * n_any,
        out_specs=jax.tree.map(lambda _: pl.BlockSpec(memory_space=pltpu.VMEM), out_shapes),
        scratch_shapes=scratch,
        compiler_params=pltpu.CompilerParams(
            vmem_limit_bytes=limit
        ),
        cost_estimate=pl.CostEstimate(flops=cost, bytes_accessed=cost, transcendentals=0),
        name=name,
    )


def in_hbm(x):
    return pltpu.with_memory_space_constraint(x, pltpu.HBM)


def sds(shape, dtype):
    return jax.ShapeDtypeStruct(shape, dtype)


def norm_forward(residual):
    average = jnp.mean(residual, axis=-1, keepdims=True)
    centred = residual - average
    inverse = lax.rsqrt(jnp.mean(centred * centred, axis=-1, keepdims=True) + norm_eps)
    return centred * inverse, inverse


def norm_backward(grad_out, normal, inverse, gain):
    scaled = grad_out * gain
    first = jnp.mean(scaled, axis=-1, keepdims=True)
    second = jnp.mean(scaled * normal, axis=-1, keepdims=True)
    return inverse * (scaled - first - normal * second)


def column_sum(x):
    return jnp.sum(x, axis=0, keepdims=True)


def head_mask(h, rows):
    lane = lax.broadcasted_iota(jnp.int32, (rows, 2 * HEAD_DIM), 1)
    return (lane // HEAD_DIM) == h


def soft_rows(q_pair, k_pair, dead, mask):
    scale = HEAD_DIM ** (-0.5)
    q_head = jnp.where(mask, q_pair, jnp.zeros_like(q_pair))
    scores = dot_nt(q_head, k_pair) * scale
    scores = jnp.where(dead, masked_score, scores)
    expo = jnp.exp(scores - jnp.max(scores, axis=-1, keepdims=True))
    return expo / jnp.sum(expo, axis=-1, keepdims=True)


def pack_kernel(where_ref, q_ref, k_ref, v_ref, o_ref, *refs):
    vectors, table_ref, b_up_ref = refs[:TB], refs[TB], refs[TB + 1]
    first_ref, second_ref, half_first_ref, half_second_ref, spread = refs[TB + 2 :]
    rows, width = q_ref.shape
    f, y = where_ref[0], where_ref[1]
    half = half_first_ref.shape[1]
    cols = pl.ds(pl.multiple_of(y * half, 128), half)
    for whole_ref, half_ref, pair in (
        (first_ref, half_first_ref, (q_ref, k_ref)),
        (second_ref, half_second_ref, (v_ref, o_ref)),
    ):
        for m, ref in enumerate(pair):
            at = slice(m * rows, (m + 1) * rows)
            half_ref[at, :] = ref[:, cols]
            whole_ref[at, :] = ref[...]
    spread[...] = jnp.zeros(spread.shape, f32)
    table = table_ref[...].astype(f32)
    for k in range(4):

        @pl.when(f == k)
        def _():
            mine = slice(k * rows, (k + 1) * rows)
            for n, ref in enumerate(vectors):
                spread[n : n + 1, mine] = ref[...].astype(f32).reshape(1, rows)
            spread[TB : TB + 2, mine] = table
            spread[BU + k : BU + k + 1, :] = b_up_ref[...].astype(f32).reshape(1, width)

    first_ref[2 * rows :, :] = spread[...].astype(bf16)
    half_first_ref[2 * rows :, :] = spread[:, cols].astype(bf16)


def put_blocks(value, f, blocks, targets, at):
    rows = value.shape[1] // 4
    for i in range(4):
        blocks[i] = value[:, i * rows : (i + 1) * rows]
    for n, target in enumerate(targets):
        target[at] = blocks[f ^ n]
        target[at + 1] = blocks[f ^ 2 ^ n]


def attend_kernel(
    where_ref,
    species_ref,
    x_ref,
    ids_ref,
    *refs,
    length,
):
    pieces, later_pieces = refs[:6], refs[6:12]
    (
        q_ref,
        k_ref,
        v_ref,
        own_ref,
        share_ref,
        n1_ref,
        inv_ref,
        low_ref,
        low_own_ref,
        low_share_ref,
        vec_ref,
        wbuf,
        vbuf,
        abuf,
        blocks,
        sems,
    ) = refs[12:]
    f = where_ref[0]
    tokens, width = x_ref.shape
    cells = tokens // length
    rows = width // 4
    vec_copies = start_rows(
        attn_plan(2 * rows, VEC_ROWS), pieces, where_ref, VEC_ROWS, vbuf, sems, 24
    )
    copies = []
    for m in range(4):
        from_pieces = pieces if m < 2 else later_pieces
        plan = attn_plan((m % 2) * rows, rows)
        copies.append(start_rows(plan, from_pieces, where_ref, rows, wbuf.at[m], sems, 6 * m))
    wait_all(vec_copies)
    vec = vbuf[0:VEC_ROWS, :].astype(f32)
    for i in range(1, 4):
        vec = vec + vbuf[i * VEC_ROWS : (i + 1) * VEC_ROWS, :].astype(f32)
    vec_ref[...] = vec
    summed = []
    for c in range(cells):
        offset = jnp.where(species_ref[c] == 1, vec[TB + 1 : TB + 2, :], vec[TB : TB + 1, :])
        summed.append(x_ref[c * length : (c + 1) * length, :].astype(f32) + offset)
    summed = jnp.concatenate(summed, axis=0)
    summed_low = summed.astype(bf16)
    put_blocks(summed_low, f, blocks, (own_ref, share_ref), 2)
    wait_all(copies[0])
    q_ref[...] = (dot(summed_low, wbuf[0]) + vec[BQ : BQ + 1, :]).astype(bf16)
    wait_all(copies[1])
    k_ref[...] = dot(summed_low, wbuf[1]).astype(bf16)
    wait_all(copies[2])
    v_ref[...] = (dot(summed_low, wbuf[2]) + vec[BV : BV + 1, :]).astype(bf16)
    pair = 2 * HEAD_DIM
    masks = [head_mask(h, length) for h in range(2)]
    for c in range(cells):
        at = slice(c * length, (c + 1) * length)
        dead = jnp.broadcast_to(ids_ref[c : c + 1, :], (length, length)) == 0
        for p in range(width // pair):
            cols = slice(p * pair, (p + 1) * pair)
            q_pair, k_pair, v_pair = q_ref[at, cols], k_ref[at, cols], v_ref[at, cols]
            total = None
            for h in range(2):
                soft = soft_rows(q_pair, k_pair, dead, masks[h]).astype(bf16)
                part = dot(soft, jnp.where(masks[h], v_pair, jnp.zeros_like(v_pair)))
                total = part if total is None else total + part
            abuf[at, cols] = total.astype(bf16)
    attended = abuf[...]
    put_blocks(attended, f, blocks, (own_ref, share_ref), 0)
    wait_all(copies[3])
    branch = dot(attended, wbuf[3]) + vec[BO : BO + 1, :]
    normal, inverse = norm_forward(summed + branch)
    n1_ref[...] = normal
    inv_ref[...] = jnp.broadcast_to(inverse, inv_ref.shape)
    low = (normal * vec[G1 : G1 + 1, :] + vec[S1 : S1 + 1, :]).astype(bf16)
    low_ref[...] = low
    put_blocks(low, f, blocks, (low_own_ref, low_share_ref), 0)


def up_kernel(where_ref, low_ref, vec_ref, *refs):
    pieces = refs[:8]
    act_ref, own_ref, near_ref, across_ref, slope_ref, wbuf, sems = refs[8:]
    f = where_ref[0]
    hidden = wbuf.shape[1]
    rows = wbuf.shape[0] // 4
    block = hidden // 4
    wait_all(start_rows(up_plan(rows), pieces, where_ref, rows, wbuf, sems, 0))
    low = low_ref[...]
    for j in range(4):
        up = dot(low, wbuf[:, j * block : (j + 1) * block]) + vec_ref[BU + j : BU + j + 1, :]
        half_cdf = 0.5 * (1.0 + lax.erf(up * (0.5**0.5)))
        density = jnp.exp(-0.5 * up * up) * 0.3989422804014327
        act_ref[j] = (up * half_cdf).astype(bf16)
        slope_ref[j] = half_cdf + up * density
    own_ref[...] = act_ref[f]
    near_ref[...] = act_ref[f ^ 1]
    across_ref[0] = act_ref[f ^ 2]
    across_ref[1] = act_ref[f ^ 3]


def down_kernel(where_ref, act_ref, n1_ref, vec_ref, cot_ref, *refs):
    pieces = refs[:10]
    out_ref, gsec_ref, glow_ref, sm_ref, wbuf, sems = refs[10:]
    rows = wbuf.shape[0] // 4
    width = wbuf.shape[1]
    copies = start_rows(down_plan(rows), pieces, where_ref, rows, wbuf, sems, 0)
    vec = vec_ref[...]
    wait_all(copies)
    branch = None
    for j in range(4):
        part = dot(act_ref[j], wbuf[j * rows : (j + 1) * rows, :])
        branch = part if branch is None else branch + part
    normed = n1_ref[...] * vec[G1 : G1 + 1, :] + vec[S1 : S1 + 1, :]
    normal, inverse = norm_forward(normed + (branch + vec[BD : BD + 1, :]))
    gain = vec[G2 : G2 + 1, :]
    out_ref[...] = (normal * gain + vec[S2 : S2 + 1, :]).astype(bf16)
    cot = cot_ref[...].astype(f32)
    grad = norm_backward(cot, normal, inverse, gain)
    gsec_ref[...] = grad
    low = grad.astype(bf16)
    glow_ref[...] = low
    sm_ref[0:1, :] = column_sum(cot * normal)
    sm_ref[1:2, :] = column_sum(cot)
    sm_ref[2:3, :] = column_sum(low.astype(f32))
    sm_ref[3:8, :] = jnp.zeros((5, width), f32)


def near_up_kernel(where_ref, own_ref, got_ref, *refs):
    rights, got_rights = refs[:4], refs[4:8]
    send_x, keep_x, send_y, keep_y = refs[8:]
    block = rights[0].shape[1]
    part = send_x.shape[1]
    low_first = where_ref[1 + UP_BITS[0]] == 0
    for slot, out in ((1, send_x), (0, keep_x)):
        for j in range(4):
            cols = slice(j * block, (j + 1) * block)
            total = dot_tn(own_ref[slot], rights[j][...]) + dot_tn(got_ref[slot], got_rights[j][...])
            total = total.astype(bf16)
            out[0, :, cols] = total[:part]
            out[1, :, cols] = total[2 * part : 3 * part]
            first, second = total[part : 2 * part], total[3 * part :]
            send_y[slot, :, cols] = jnp.where(low_first, second, first)
            keep_y[slot, :, cols] = jnp.where(low_first, first, second)


def near_attn_kernel(where_ref, own_ref, got_ref, *refs):
    rights, got_rights = refs[:4], refs[4:8]
    send_x, keep_x, send_y, keep_y = refs[8:]
    low_y = where_ref[1] == 0

    def block(left, n):
        total = dot_tn(own_ref[left], rights[n][...]) + dot_tn(got_ref[left], got_rights[n][...])
        return total.astype(bf16)

    for slot, ref in ((1, send_x), (0, keep_x)):
        ref[0] = block(slot, 0)
        ref[1] = block(2 + slot, 1)
        query, key = block(2 + slot, 2), block(2 + slot, 3)
        send_y[slot] = jnp.where(low_y, key, query)
        keep_y[slot] = jnp.where(low_y, query, key)


def down_grad_kernel(where_ref, *refs):
    lefts, rights, outs = refs[:4], refs[4:8], refs[8:]
    mine = where_ref[1 + DOWN_BITS[0]]
    rows = outs[0].shape[0]
    for half, out in ((1 - mine, outs[0]), (mine, outs[1])):
        cols = pl.ds(pl.multiple_of(half * rows, 128), rows)
        total = None
        for n, (left, right) in enumerate(zip(lefts, rights)):
            part = dot_tn(left[0, :, cols] if n == 2 else left[:, cols], right[...])
            total = part if total is None else total + part
        out[...] = total.astype(bf16)


def hidden_back_kernel(where_ref, glow_ref, slope_ref, *refs):
    pieces = refs[:10]
    guis, sm_ref, wbuf, sems = refs[10:14], refs[14], refs[15], refs[16]
    rows = wbuf.shape[0] // 4
    width = wbuf.shape[1]
    wait_all(start_rows(down_plan(rows), pieces, where_ref, rows, wbuf, sems, 0))
    glow = glow_ref[...]
    for j in range(4):
        grad = dot_nt(glow, wbuf[j * rows : (j + 1) * rows, :]) * slope_ref[j]
        low = grad.astype(bf16)
        guis[j][...] = low
        sm_ref[j : j + 1, :] = column_sum(low.astype(f32))
    sm_ref[4:8, :] = jnp.zeros((4, rows), f32)


def norm_back_kernel(where_ref, gsec_ref, n1_ref, inv_ref, vec_ref, *refs):
    guis, pieces, attn_pieces = refs[:4], refs[4:12], refs[12:18]
    gres_ref, gbr_ref, gatt_ref, sm_ref, wbuf, obuf, sems = refs[18:]
    rows = wbuf.shape[0] // 4
    hidden = wbuf.shape[1]
    width = obuf.shape[1]
    copies = start_rows(up_plan(rows), pieces, where_ref, rows, wbuf, sems, 0)
    out_copies = start_rows(attn_plan(rows, rows), attn_pieces, where_ref, rows, obuf, sems, 8)
    wait_all(copies)
    block = hidden // 4
    grad_normed = gsec_ref[...]
    for j in range(4):
        grad_normed = grad_normed + dot_nt(guis[j][...], wbuf[:, j * block : (j + 1) * block])
    normal = n1_ref[...]
    grad = norm_backward(grad_normed, normal, inv_ref[:, 0:1], vec_ref[G1 : G1 + 1, :])
    gres_ref[...] = grad
    low = grad.astype(bf16)
    gbr_ref[...] = low
    sm_ref[0:1, :] = column_sum(grad_normed * normal)
    sm_ref[1:2, :] = column_sum(grad_normed)
    sm_ref[2:3, :] = column_sum(low.astype(f32))
    sm_ref[3:8, :] = jnp.zeros((5, width), f32)
    wait_all(out_copies)
    gatt_ref[...] = dot_nt(low, obuf[...]).astype(bf16)


def attend_back_kernel(q_ref, k_ref, v_ref, gatt_ref, ids_ref, gq_ref, gk_ref, gv_ref, *, length):
    tokens, width = q_ref.shape
    cells = tokens // length
    scale = HEAD_DIM ** (-0.5)
    pair = 2 * HEAD_DIM
    masks = [head_mask(h, length) for h in range(2)]
    for c in range(cells):
        at = slice(c * length, (c + 1) * length)
        dead = jnp.broadcast_to(ids_ref[c : c + 1, :], (length, length)) == 0
        for p in range(width // pair):
            cols = slice(p * pair, (p + 1) * pair)
            q_pair, k_pair, v_pair = q_ref[at, cols], k_ref[at, cols], v_ref[at, cols]
            g_pair = gatt_ref[at, cols]
            zero = jnp.zeros_like(q_pair)
            gq = gk = gv = jnp.zeros((length, pair), f32)
            for h in range(2):
                mask = masks[h]
                soft = soft_rows(q_pair, k_pair, dead, mask)
                g_head = jnp.where(mask, g_pair, zero)
                grad_soft = dot_nt(g_head, v_pair)
                inner = jnp.sum(soft * grad_soft, axis=-1, keepdims=True)
                grad_scores = (soft * (grad_soft - inner)).astype(bf16)
                gv = gv + dot_tn(soft.astype(bf16), g_head)
                gq = gq + dot(grad_scores, jnp.where(mask, k_pair, zero))
                gk = gk + dot_tn(grad_scores, jnp.where(mask, q_pair, zero))
            gq_ref[at, cols] = (gq * scale).astype(bf16)
            gk_ref[at, cols] = (gk * scale).astype(bf16)
            gv_ref[at, cols] = gv.astype(bf16)


def input_back_kernel(
    where_ref, species_ref, gres_ref, gq_ref, gk_ref, gv_ref, sm2_ref, smu_ref, sm1_ref, *refs,
    length,
):
    pieces, later_pieces = refs[:6], refs[6:12]
    gin_ref, sm_ref, wbuf, sems = refs[12:]
    tokens, width = gres_ref.shape
    rows = width // 4
    copies = []
    for m in range(3):
        from_pieces = pieces if m < 2 else later_pieces
        plan = attn_plan((m % 2) * rows, rows)
        copies.append(start_rows(plan, from_pieces, where_ref, rows, wbuf.at[m], sems, 6 * m))
    sm_ref[BQ : BQ + 1, :] = column_sum(gq_ref[...].astype(f32))
    sm_ref[BV : BV + 1, :] = column_sum(gv_ref[...].astype(f32))
    sm_ref[BO : BO + 1, :] = sm1_ref[2:3, :]
    sm_ref[G1 : G1 + 2, :] = sm1_ref[0:2, :]
    sm_ref[BD : BD + 1, :] = sm2_ref[2:3, :]
    sm_ref[G2 : G2 + 2, :] = sm2_ref[0:2, :]
    sm_ref[BU : BU + 4, :] = smu_ref[0:4, :]
    sm_ref[BU + 4 : VEC_ROWS, :] = jnp.zeros((VEC_ROWS - BU - 4, width), f32)
    total = gres_ref[...]
    for m, grad in enumerate((gq_ref, gk_ref, gv_ref)):
        wait_all(copies[m])
        total = total + dot_nt(grad[...], wbuf[m])
    gin_ref[...] = total.astype(bf16)
    for s in range(2):
        row = jnp.zeros((1, width), f32)
        for c in range(tokens // length):
            cell = column_sum(total[c * length : (c + 1) * length, :])
            row = row + jnp.where(species_ref[c] == s, cell, jnp.zeros_like(cell))
        sm_ref[TB + s : TB + s + 1, :] = row


def half_rows(x, bit):
    rows = x.shape[-2] // 2
    return lax.dynamic_slice_in_dim(x, bit * rows, rows, x.ndim - 2)


def add(a, b):
    return (a.astype(f32) + b.astype(f32)).astype(bf16)


def two_way_chain(send_x, keep_x, send_b, keep_b, dp_index, bits, steps, b_first):
    p, q = [(dp_index >> bit) & 1 for bit in bits]
    one, two = [1 << bit for bit in bits]
    got_x = swap(send_x, "fsdp", 2)
    got_b = swap(send_b, "dp", one)
    last = send_b
    for over_x in (False, True) if b_first else (True, False):
        if over_x:
            got_x = yield got_x, last
            last = jnp.where(p == 0, add(keep_x[1], got_x[1]), add(keep_x[0], got_x[0]))
            take = jnp.where(p == 0, add(keep_x[0], got_x[0]), add(keep_x[1], got_x[1]))
            got_take = swap(last, "dp", one)
        else:
            got_b = yield got_b, last
            last = add(keep_b[1], got_b[1])
            rest = add(keep_b[0], got_b[0])
            got_rest = swap(last, "fsdp", 2)
    got_take = yield got_take, last
    first = add(take, got_take)
    got_rest = yield got_rest, first
    second = add(rest, got_rest)
    send = jnp.where(q == 0, second, first)
    keep = jnp.where(q == 0, first, second)
    got = yield swap(send, "dp", two), send
    total = add(keep, got)
    for step in steps[:-1]:
        bit = (dp_index >> step) & 1
        send = half_rows(total, 1 - bit)
        got = yield swap(send, "dp", 1 << step), send
        total = add(half_rows(total, bit), got)
    got = yield swap(total, "dp", 1 << steps[-1]), total
    total = add(total, got)
    for step in reversed(steps[:-1]):
        other = yield swap(total, "dp", 1 << step), total
        total = join_rows(total, other, dp_index, step)
    other = yield swap(total, "dp", two), total
    mine = jnp.stack([jnp.where(q == 0, total, other), jnp.where(q == 0, other, total)])
    other = yield swap(mine, "dp", one), mine
    return jnp.where(p == 0, mine, other), jnp.where(p == 0, other, mine)


def join_rows(total, other, dp_index, step):
    return jnp.where(
        (dp_index >> step) & 1 == 0,
        jnp.concatenate([total, other], axis=0),
        jnp.concatenate([other, total], axis=0),
    )


def halving_chain(send, keep, dp_index, steps):
    got = yield swap(send, "dp", 1 << steps[0]), send
    for step in steps[1:-1]:
        bit = (dp_index >> step) & 1
        send = add(half_rows(keep, 1 - bit), half_rows(got, 1 - bit))
        keep = add(half_rows(keep, bit), half_rows(got, bit))
        got = yield swap(send, "dp", 1 << step), send
    total = add(keep, got)
    got = yield swap(total, "dp", 1 << steps[-1]), total
    total = add(total, got)
    for step in reversed(steps[:-1]):
        other = yield swap(total, "dp", 1 << step), total
        total = join_rows(total, other, dp_index, step)
    return total


def whole_chain(total, steps):
    for axis, distance in (("fsdp", 1), ("fsdp", 2)) + tuple(("dp", 1 << step) for step in steps):
        got = yield swap(total, axis, distance), total
        total = total + got
    return total


class Turns:
    def __init__(self):
        self.pending, self.done = {}, {}

    def add(self, name, chain):
        self.pending[name] = next(chain)[0], chain

    def take(self, names, token):
        for name in names:
            if name in self.pending:
                value, chain = self.pending[name]
                try:
                    value, token = chain.send(tie(value, token))
                    self.pending[name] = value, chain
                except StopIteration as stop:
                    self.done[name] = stop.value
                    del self.pending[name]
        return token


def local(
    inputs,
    species,
    gene_ids,
    cotangent,
    table,
    w_query,
    b_query,
    w_key,
    w_value,
    b_value,
    w_out,
    b_out,
    gain_one,
    shift_one,
    w_up,
    b_up,
    w_down,
    b_down,
    gain_two,
    shift_two,
):
    cells, length, width = inputs.shape
    tokens = cells * length
    rows = w_query.shape[0]
    hidden = w_up.shape[1]
    shard_hidden = w_down.shape[0]
    shards = lax.axis_size("fsdp")
    f = lax.axis_index("fsdp")
    d = lax.axis_index("dp")
    y_bit = d & 1
    where = jnp.stack([f, y_bit, (d >> 1) & 1]).astype(jnp.int32)
    order = tuple(range((lax.axis_size("dp") - 1).bit_length()))

    z_bit = (d >> 1) & 1
    first_own, second_own, first_half, second_half = call(
        pack_kernel,
        (
            sds((2 * rows + VEC_ROWS, width), bf16),
            sds((2 * rows, width), bf16),
            sds((2 * rows + VEC_ROWS, width // 2), bf16),
            sds((2 * rows, width // 2), bf16),
        ),
        1,
        6 + TB,
        0,
        [pltpu.VMEM((VEC_ROWS, width), f32)],
        "pack",
        resident=False,
        limit=LARGE_VMEM_LIMIT,
    )(
        where,
        w_query,
        w_key,
        w_value,
        w_out,
        b_query,
        b_value,
        b_out,
        gain_one,
        shift_one,
        b_down,
        gain_two,
        shift_two,
        table,
        b_up,
    )

    def relays(half, axis_bit):
        across = swap(half, "fsdp", 2)
        return across, swap(across, "dp", axis_bit)

    def with_core(across, relayed, when=None):
        if when is not None:
            across, relayed = tie(across, when), tie(relayed, when)
        return across, relayed, swap(across, "fsdp", 1), swap(relayed, "fsdp", 1)

    first = relays(first_half, 1)
    second = relays(tie(second_half, first_half), 1)
    up_top = relays(tie(half_columns(w_up[: rows // 2], z_bit), first[0]), 2)
    up_rest = swap(tie(w_up[rows // 2 :], first[0]), "fsdp", 2)
    attn_first = (first_own, swap(first_own, "fsdp", 1), *with_core(*first))
    attn_second = (second_own, swap(second_own, "fsdp", 1), *with_core(*second))
    attn_first = tuple(map(in_hbm, attn_first))
    attn_second = tuple(map(in_hbm, attn_second))
    down_core = swap(w_down, "fsdp", 1)
    up_core = swap(w_up, "fsdp", 1)
    top = shard_hidden // 2
    down_top = swap(tie(half_columns(w_down[:top], y_bit), up_top[0]), "fsdp", 2)
    down_rest = swap(tie(half_columns(w_down[top:], z_bit), up_top[0]), "fsdp", 2)

    x_rows = inputs.reshape(tokens, width)
    cot_rows = cotangent.reshape(tokens, width)
    flat_low = sds((tokens, width), bf16)
    flat = sds((tokens, width), f32)
    small = sds((8, width), f32)
    q, k, v, own_attn, share_attn, n1, inv1, low, low_own, low_share, vec = call(
        partial(attend_kernel, length=length),
        (
            flat_low,
            flat_low,
            flat_low,
            pltpu.HBM((4, tokens, rows), bf16),
            pltpu.HBM((4, tokens, rows), bf16),
            flat,
            sds((tokens, 128), f32),
            flat_low,
            pltpu.HBM((2, tokens, rows), bf16),
            pltpu.HBM((2, tokens, rows), bf16),
            sds((VEC_ROWS, width), f32),
        ),
        2,
        2,
        12,
        [
            pltpu.VMEM((4, width, width), bf16),
            pltpu.VMEM((4 * VEC_ROWS, width), bf16),
            pltpu.VMEM((tokens, width), bf16),
            pltpu.VMEM((4, tokens, rows), bf16),
            pltpu.SemaphoreType.DMA((30,)),
        ],
        "attend",
        ATTEND_COST,
    )(where, species, x_rows, gene_ids, *attn_first, *attn_second)
    up_late = tie(up_rest, q)
    up = (w_up, up_core, *with_core(*up_top, q), up_late, swap(up_late, "fsdp", 1))
    down_top = tie(down_top, q)
    down_top = (down_top, swap(down_top, "dp", 1))
    act, act_own, act_near, act_across, slope = call(
        up_kernel,
        (
            sds((shards, tokens, shard_hidden), bf16),
            *(pltpu.HBM((tokens, shard_hidden), bf16),) * 2,
            pltpu.HBM((2, tokens, shard_hidden), bf16),
            sds((shards, tokens, shard_hidden), f32),
        ),
        1,
        2,
        8,
        [pltpu.VMEM((width, hidden), bf16), pltpu.SemaphoreType.DMA((8,))],
        "up",
    )(where, low, vec, *up)
    down_rest = tie(down_rest, act_own)
    down_rest = (down_rest, swap(down_rest, "dp", 2))
    down = (w_down, down_core, *with_core(*down_top, act_own), *with_core(*down_rest))
    output, gsec, glow, sm2 = call(
        down_kernel,
        (flat_low, flat, flat_low, small),
        1,
        4,
        10,
        [pltpu.VMEM((hidden, width), bf16), pltpu.SemaphoreType.DMA((10,))],
        "down",
    )(where, act, n1, vec, cot_rows, *down)
    act_got = swap(act_across, "fsdp", 2)
    glow_across = swap(glow, "fsdp", 2)
    *guis, smu = call(
        hidden_back_kernel,
        (*(sds((tokens, shard_hidden), bf16),) * 4, sds((8, shard_hidden), f32)),
        1,
        2,
        10,
        [pltpu.VMEM((hidden, width), bf16), pltpu.SemaphoreType.DMA((10,))],
        "hidden_back",
    )(where, glow, slope, *down)
    guis_got = [swap(part, "fsdp", 1) for part in guis]
    gres, gbr, gatt, sm1 = call(
        norm_back_kernel,
        (pltpu.HBM(flat.shape, f32), flat_low, flat_low, small),
        1,
        8,
        14,
        [
            pltpu.VMEM((width, hidden), bf16),
            pltpu.VMEM((width, width), bf16),
            pltpu.SemaphoreType.DMA((14,)),
        ],
        "norm_back",
    )(where, gsec, n1, inv1, vec, *guis, *up, *attn_second)
    part = pltpu.HBM((2, rows // 4, hidden), bf16)
    up_parts = call(near_up_kernel, (part,) * 4, 1, 10, 0, [], "near_up", resident=False)(
        tie(where, gbr), in_hbm(low_own), in_hbm(swap(low_share, "fsdp", 1)), *guis, *guis_got
    )
    gq, gk, gv = call(
        partial(attend_back_kernel, length=length),
        (flat_low, flat_low, flat_low),
        0,
        5,
        0,
        [],
        "attend_back",
    )(q, k, v, tie(gatt, up_parts[0]), gene_ids)
    act_all = (
        act_own,
        swap(tie(act_near, gbr), "fsdp", 1),
        act_got,
        swap(tie(act_got, gbr)[1], "fsdp", 1),
    )
    glow_all = (
        glow,
        swap(tie(glow, gbr), "fsdp", 1),
        glow_across,
        swap(tie(glow_across, gq), "fsdp", 1),
    )
    turns = Turns()
    turns.add("U", two_way_chain(*up_parts, d, UP_BITS, order[2:], UP_STRIPS_FIRST))
    rights = [gbr, gv, gq, gk]
    rights_got = [swap(right, "fsdp", 1) for right in rights]
    down_half = pltpu.HBM((shard_hidden // 2, width), bf16)
    send_down, keep_down = call(down_grad_kernel, (down_half,) * 2, 1, 8, 0, [], "down_grad", resident=False)(
        tie(where, gq), *map(in_hbm, act_all), glow, *map(in_hbm, glow_all[1:])
    )
    turns.add("D", halving_chain(send_down, keep_down, d, DOWN_BITS + order[2:]))
    token = turns.take(EARLY_TURNS, keep_down)
    pair = pltpu.HBM((2, rows, width), bf16)
    attn_parts = call(near_attn_kernel, (pair,) * 4, 1, 10, 0, [], "near_attn", resident=False)(
        tie(where, keep_down, token), in_hbm(own_attn), in_hbm(swap(share_attn, "fsdp", 1)), *rights, *map(in_hbm, rights_got)
    )
    turns.add("A", two_way_chain(*attn_parts, d, (0, 1), order[2:], False))
    token = turns.take(MIDDLE_TURNS, attn_parts[0])
    gin, sm = call(
        partial(input_back_kernel, length=length),
        (flat_low, sds((VEC_ROWS, width), f32)),
        2,
        7,
        12,
        [pltpu.VMEM((3, width, width), bf16), pltpu.SemaphoreType.DMA((18,))],
        "input_back",
        resident=False,
    )(
        tie(where, token),
        species,
        gres,
        gq,
        gk,
        gv,
        sm2,
        smu,
        sm1,
        *attn_first,
        *attn_second,
    )
    turns.add("S", whole_chain(sm, order))
    token = turns.take(TURNS, token)
    while turns.pending:
        token = turns.take(tuple(turns.pending), token)
    grad_up = jnp.stack(turns.done["U"]).reshape(rows, hidden)
    grad_down = turns.done["D"]
    low_attn, high_attn = turns.done["A"]
    sm = turns.done["S"]

    mine = lax.dynamic_slice_in_dim(sm, f * rows, rows, 1)
    b_up_grad = lax.dynamic_slice_in_dim(sm, BU + f, 1, 0)[0]

    return (
        output.reshape(inputs.shape),
        gin.reshape(inputs.shape),
        mine[TB : TB + 2],
        low_attn[1].astype(f32),
        mine[BQ],
        high_attn[1].astype(f32),
        high_attn[0].astype(f32),
        mine[BV],
        low_attn[0].astype(f32),
        mine[BO],
        mine[G1],
        mine[S1],
        grad_up.astype(f32),
        b_up_grad,
        grad_down.astype(f32),
        mine[BD],
        mine[G2],
        mine[S2],
    )


def solution(mesh):
    cells = P(("dp", "fsdp"), None, None)
    vector = P("fsdp")
    matrix = P("fsdp", None)
    table = P(None, "fsdp")
    return jax.shard_map(
        local,
        mesh=mesh,
        in_specs=(
            cells,
            P(("dp", "fsdp")),
            P(("dp", "fsdp"), None),
            cells,
            table,
            matrix,
            vector,
            matrix,
            matrix,
            vector,
            matrix,
            vector,
            vector,
            vector,
            matrix,
            vector,
            matrix,
            vector,
            vector,
            vector,
        ),
        out_specs=(
            cells,
            cells,
            table,
            matrix,
            vector,
            matrix,
            matrix,
            vector,
            matrix,
            vector,
            vector,
            vector,
            matrix,
            vector,
            matrix,
            vector,
            vector,
            vector,
        ),
        check_vma=False,
    )
```

```python
from functools import partial

import jax
import jax.numpy as jnp
from jax import lax
from jax.experimental import pallas as pl
from jax.experimental.pallas import tpu as pltpu
from jax.sharding import PartitionSpec as P

HEAD_DIM = 64
norm_eps = 1e-12
masked_score = -1e30
f32 = jnp.float32
bf16 = jnp.bfloat16

BQ, BV, BO, G1, S1, BD, G2, S2, TB, BU = 0, 1, 2, 3, 4, 5, 6, 7, 8, 10
VEC_ROWS = 16
EARLY_TURNS = ""
MIDDLE_TURNS = "UU"
UP_STRIPS_FIRST = False
TURNS = "DUSASUADAASUDASUDASUUADA"
UP_BITS = (1, 0)
DOWN_BITS = (0, 1)
COST = 1024
ATTEND_COST = 1024
VMEM_LIMIT = 16 * 1024 * 1024
LARGE_VMEM_LIMIT = 56 * 1024 * 1024


def dot(a, b):
    return jnp.dot(a, b, preferred_element_type=f32)


def dot_nt(a, b):
    return lax.dot_general(a, b, (((1,), (1,)), ((), ())), preferred_element_type=f32)


def dot_tn(a, b):
    return lax.dot_general(a, b, (((0,), (0,)), ((), ())), preferred_element_type=f32)


def swap(x, axis, distance):
    count = lax.axis_size(axis)
    with jax.named_scope(f"swap_{axis}{distance}"):
        return lax.ppermute(x, axis, [(i, i ^ distance) for i in range(count)])


def half_columns(x, bit):
    width = x.shape[1] // 2
    return lax.dynamic_slice_in_dim(x, bit * width, width, 1)


def tie(x, *others):
    return lax.optimization_barrier((x,) + others)[0]


def halved(first, rows, top, bit):
    return [
        (first, top, rows, 2, bit, 0),
        (first + 1, top, rows, 2, bit, 1),
        (first + 2, top, rows, 3, bit, 0),
        (first + 3, top, rows, 3, bit, 1),
    ]


def start_rows(plan, pieces, where_ref, shard_rows, target, sems, base):
    width = target.shape[1]
    half = width // 2
    copies = []
    for n, (piece, first, rows, distance, bit, other, *at) in enumerate(plan):
        row = pl.multiple_of((where_ref[0] ^ distance) * shard_rows + (at[0] if at else 0), 8)
        if bit is None:
            cols = pl.ds(0, width)
        else:
            side = where_ref[bit]
            cols = pl.ds(pl.multiple_of((1 - side if other else side) * half, 128), half)
        copy = pltpu.make_async_copy(
            pieces[piece].at[pl.ds(first, rows), :],
            target.at[pl.ds(row, rows), cols],
            sems.at[base + n],
        )
        copy.start()
        copies.append(copy)
    return copies


def attn_plan(first, rows):
    return [(0, first, rows, 0, None, 0), (1, first, rows, 1, None, 0)] + halved(2, rows, first, 1)


def up_plan(rows):
    half = rows // 2
    plan = [(0, 0, rows, 0, None, 0), (1, 0, rows, 1, None, 0)] + halved(2, half, 0, 2)
    return plan + [(6, 0, half, 2, None, 0, half), (7, 0, half, 3, None, 0, half)]


def down_plan(rows):
    half = rows // 2
    plan = [(0, 0, rows, 0, None, 0), (1, 0, rows, 1, None, 0)] + halved(2, half, 0, 1)
    return plan + [copy + (half,) for copy in halved(6, half, 0, 2)]


def wait_all(copies):
    for copy in copies:
        copy.wait()


def call(kernel, out_shapes, n_smem, n_vmem, n_any, scratch, name, cost=COST, resident=True, limit=VMEM_LIMIT):
    if resident:
        out_shapes = jax.tree.map(
            lambda out: pltpu.VMEM(out.shape, out.dtype)
            if isinstance(out, jax.ShapeDtypeStruct)
            else out,
            out_shapes,
        )
    return pl.pallas_call(
        kernel,
        out_shape=out_shapes,
        in_specs=[pl.BlockSpec(memory_space=pltpu.SMEM)] * n_smem
        + [pl.BlockSpec(memory_space=pltpu.VMEM)] * n_vmem
        + [pl.BlockSpec(memory_space=pl.ANY)] * n_any,
        out_specs=jax.tree.map(lambda _: pl.BlockSpec(memory_space=pltpu.VMEM), out_shapes),
        scratch_shapes=scratch,
        compiler_params=pltpu.CompilerParams(
            vmem_limit_bytes=limit
        ),
        cost_estimate=pl.CostEstimate(flops=cost, bytes_accessed=cost, transcendentals=0),
        name=name,
    )


def in_hbm(x):
    return pltpu.with_memory_space_constraint(x, pltpu.HBM)


def sds(shape, dtype):
    return jax.ShapeDtypeStruct(shape, dtype)


def norm_forward(residual):
    average = jnp.mean(residual, axis=-1, keepdims=True)
    centred = residual - average
    inverse = lax.rsqrt(jnp.mean(centred * centred, axis=-1, keepdims=True) + norm_eps)
    return centred * inverse, inverse


def norm_backward(grad_out, normal, inverse, gain):
    scaled = grad_out * gain
    first = jnp.mean(scaled, axis=-1, keepdims=True)
    second = jnp.mean(scaled * normal, axis=-1, keepdims=True)
    return inverse * (scaled - first - normal * second)


def column_sum(x):
    return jnp.sum(x, axis=0, keepdims=True)


def head_mask(h, rows):
    lane = lax.broadcasted_iota(jnp.int32, (rows, 2 * HEAD_DIM), 1)
    return (lane // HEAD_DIM) == h


def soft_rows(q_pair, k_pair, dead, mask):
    scale = HEAD_DIM ** (-0.5)
    q_head = jnp.where(mask, q_pair, jnp.zeros_like(q_pair))
    scores = dot_nt(q_head, k_pair) * scale
    scores = jnp.where(dead, masked_score, scores)
    expo = jnp.exp(scores - jnp.max(scores, axis=-1, keepdims=True))
    return expo / jnp.sum(expo, axis=-1, keepdims=True)


def pack_kernel(where_ref, q_ref, k_ref, v_ref, o_ref, *refs):
    vectors, table_ref, b_up_ref = refs[:TB], refs[TB], refs[TB + 1]
    first_ref, second_ref, half_first_ref, half_second_ref, spread = refs[TB + 2 :]
    rows, width = q_ref.shape
    f, y = where_ref[0], where_ref[1]
    half = half_first_ref.shape[1]
    cols = pl.ds(pl.multiple_of(y * half, 128), half)
    for whole_ref, half_ref, pair in (
        (first_ref, half_first_ref, (q_ref, k_ref)),
        (second_ref, half_second_ref, (v_ref, o_ref)),
    ):
        for m, ref in enumerate(pair):
            at = slice(m * rows, (m + 1) * rows)
            half_ref[at, :] = ref[:, cols]
            whole_ref[at, :] = ref[...]
    spread[...] = jnp.zeros(spread.shape, f32)
    table = table_ref[...].astype(f32)
    for k in range(4):

        @pl.when(f == k)
        def _():
            mine = slice(k * rows, (k + 1) * rows)
            for n, ref in enumerate(vectors):
                spread[n : n + 1, mine] = ref[...].astype(f32).reshape(1, rows)
            spread[TB : TB + 2, mine] = table
            spread[BU + k : BU + k + 1, :] = b_up_ref[...].astype(f32).reshape(1, width)

    first_ref[2 * rows :, :] = spread[...].astype(bf16)
    half_first_ref[2 * rows :, :] = spread[:, cols].astype(bf16)


def put_blocks(value, f, blocks, targets, at):
    rows = value.shape[1] // 4
    for i in range(4):
        blocks[i] = value[:, i * rows : (i + 1) * rows]
    for n, target in enumerate(targets):
        target[at] = blocks[f ^ n]
        target[at + 1] = blocks[f ^ 2 ^ n]


def attend_kernel(
    where_ref,
    species_ref,
    x_ref,
    ids_ref,
    *refs,
    length,
):
    pieces, later_pieces = refs[:6], refs[6:12]
    (
        q_ref,
        k_ref,
        v_ref,
        own_ref,
        share_ref,
        n1_ref,
        inv_ref,
        low_ref,
        low_own_ref,
        low_share_ref,
        vec_ref,
        wbuf,
        vbuf,
        abuf,
        blocks,
        sems,
    ) = refs[12:]
    f = where_ref[0]
    tokens, width = x_ref.shape
    cells = tokens // length
    rows = width // 4
    vec_copies = start_rows(
        attn_plan(2 * rows, VEC_ROWS), pieces, where_ref, VEC_ROWS, vbuf, sems, 24
    )
    copies = []
    for m in range(4):
        from_pieces = pieces if m < 2 else later_pieces
        plan = attn_plan((m % 2) * rows, rows)
        copies.append(start_rows(plan, from_pieces, where_ref, rows, wbuf.at[m], sems, 6 * m))
    wait_all(vec_copies)
    vec = vbuf[0:VEC_ROWS, :].astype(f32)
    for i in range(1, 4):
        vec = vec + vbuf[i * VEC_ROWS : (i + 1) * VEC_ROWS, :].astype(f32)
    vec_ref[...] = vec
    summed = []
    for c in range(cells):
        offset = jnp.where(species_ref[c] == 1, vec[TB + 1 : TB + 2, :], vec[TB : TB + 1, :])
        summed.append(x_ref[c * length : (c + 1) * length, :].astype(f32) + offset)
    summed = jnp.concatenate(summed, axis=0)
    summed_low = summed.astype(bf16)
    put_blocks(summed_low, f, blocks, (own_ref, share_ref), 2)
    wait_all(copies[0])
    q_ref[...] = (dot(summed_low, wbuf[0]) + vec[BQ : BQ + 1, :]).astype(bf16)
    wait_all(copies[1])
    k_ref[...] = dot(summed_low, wbuf[1]).astype(bf16)
    wait_all(copies[2])
    v_ref[...] = (dot(summed_low, wbuf[2]) + vec[BV : BV + 1, :]).astype(bf16)
    pair = 2 * HEAD_DIM
    masks = [head_mask(h, length) for h in range(2)]
    for c in range(cells):
        at = slice(c * length, (c + 1) * length)
        dead = jnp.broadcast_to(ids_ref[c : c + 1, :], (length, length)) == 0
        for p in range(width // pair):
            cols = slice(p * pair, (p + 1) * pair)
            q_pair, k_pair, v_pair = q_ref[at, cols], k_ref[at, cols], v_ref[at, cols]
            total = None
            for h in range(2):
                soft = soft_rows(q_pair, k_pair, dead, masks[h]).astype(bf16)
                part = dot(soft, jnp.where(masks[h], v_pair, jnp.zeros_like(v_pair)))
                total = part if total is None else total + part
            abuf[at, cols] = total.astype(bf16)
    attended = abuf[...]
    put_blocks(attended, f, blocks, (own_ref, share_ref), 0)
    wait_all(copies[3])
    branch = dot(attended, wbuf[3]) + vec[BO : BO + 1, :]
    normal, inverse = norm_forward(summed + branch)
    n1_ref[...] = normal
    inv_ref[...] = jnp.broadcast_to(inverse, inv_ref.shape)
    low = (normal * vec[G1 : G1 + 1, :] + vec[S1 : S1 + 1, :]).astype(bf16)
    low_ref[...] = low
    put_blocks(low, f, blocks, (low_own_ref, low_share_ref), 0)


def up_kernel(where_ref, low_ref, vec_ref, *refs):
    pieces = refs[:8]
    act_ref, own_ref, near_ref, across_ref, slope_ref, wbuf, sems = refs[8:]
    f = where_ref[0]
    hidden = wbuf.shape[1]
    rows = wbuf.shape[0] // 4
    block = hidden // 4
    wait_all(start_rows(up_plan(rows), pieces, where_ref, rows, wbuf, sems, 0))
    low = low_ref[...]
    for j in range(4):
        up = dot(low, wbuf[:, j * block : (j + 1) * block]) + vec_ref[BU + j : BU + j + 1, :]
        half_cdf = 0.5 * (1.0 + lax.erf(up * (0.5**0.5)))
        density = jnp.exp(-0.5 * up * up) * 0.3989422804014327
        act_ref[j] = (up * half_cdf).astype(bf16)
        slope_ref[j] = half_cdf + up * density
    own_ref[...] = act_ref[f]
    near_ref[...] = act_ref[f ^ 1]
    across_ref[0] = act_ref[f ^ 2]
    across_ref[1] = act_ref[f ^ 3]


def down_kernel(where_ref, act_ref, n1_ref, vec_ref, cot_ref, *refs):
    pieces = refs[:10]
    out_ref, gsec_ref, glow_ref, sm_ref, wbuf, sems = refs[10:]
    rows = wbuf.shape[0] // 4
    width = wbuf.shape[1]
    copies = start_rows(down_plan(rows), pieces, where_ref, rows, wbuf, sems, 0)
    vec = vec_ref[...]
    wait_all(copies)
    branch = None
    for j in range(4):
        part = dot(act_ref[j], wbuf[j * rows : (j + 1) * rows, :])
        branch = part if branch is None else branch + part
    normed = n1_ref[...] * vec[G1 : G1 + 1, :] + vec[S1 : S1 + 1, :]
    normal, inverse = norm_forward(normed + (branch + vec[BD : BD + 1, :]))
    gain = vec[G2 : G2 + 1, :]
    out_ref[...] = (normal * gain + vec[S2 : S2 + 1, :]).astype(bf16)
    cot = cot_ref[...].astype(f32)
    grad = norm_backward(cot, normal, inverse, gain)
    gsec_ref[...] = grad
    low = grad.astype(bf16)
    glow_ref[...] = low
    sm_ref[0:1, :] = column_sum(cot * normal)
    sm_ref[1:2, :] = column_sum(cot)
    sm_ref[2:3, :] = column_sum(low.astype(f32))
    sm_ref[3:8, :] = jnp.zeros((5, width), f32)


def near_up_kernel(where_ref, own_ref, got_ref, *refs):
    rights, got_rights = refs[:4], refs[4:8]
    send_x, keep_x, send_y, keep_y = refs[8:]
    block = rights[0].shape[1]
    part = send_x.shape[1]
    low_first = where_ref[1 + UP_BITS[0]] == 0
    for slot, out in ((1, send_x), (0, keep_x)):
        for j in range(4):
            cols = slice(j * block, (j + 1) * block)
            total = dot_tn(own_ref[slot], rights[j][...]) + dot_tn(got_ref[slot], got_rights[j][...])
            total = total.astype(bf16)
            out[0, :, cols] = total[:part]
            out[1, :, cols] = total[2 * part : 3 * part]
            first, second = total[part : 2 * part], total[3 * part :]
            send_y[slot, :, cols] = jnp.where(low_first, second, first)
            keep_y[slot, :, cols] = jnp.where(low_first, first, second)


def near_attn_kernel(where_ref, own_ref, got_ref, *refs):
    rights, got_rights = refs[:4], refs[4:8]
    send_x, keep_x, send_y, keep_y = refs[8:]
    low_y = where_ref[1] == 0

    def block(left, n):
        total = dot_tn(own_ref[left], rights[n][...]) + dot_tn(got_ref[left], got_rights[n][...])
        return total.astype(bf16)

    for slot, ref in ((1, send_x), (0, keep_x)):
        ref[0] = block(slot, 0)
        ref[1] = block(2 + slot, 1)
        query, key = block(2 + slot, 2), block(2 + slot, 3)
        send_y[slot] = jnp.where(low_y, key, query)
        keep_y[slot] = jnp.where(low_y, query, key)


def down_grad_kernel(where_ref, *refs):
    lefts, rights, outs = refs[:4], refs[4:8], refs[8:]
    mine = where_ref[1 + DOWN_BITS[0]]
    rows = outs[0].shape[0]
    for half, out in ((1 - mine, outs[0]), (mine, outs[1])):
        cols = pl.ds(pl.multiple_of(half * rows, 128), rows)
        total = None
        for n, (left, right) in enumerate(zip(lefts, rights)):
            part = dot_tn(left[0, :, cols] if n == 2 else left[:, cols], right[...])
            total = part if total is None else total + part
        out[...] = total.astype(bf16)


def hidden_back_kernel(where_ref, glow_ref, slope_ref, *refs):
    pieces = refs[:10]
    guis, sm_ref, wbuf, sems = refs[10:14], refs[14], refs[15], refs[16]
    rows = wbuf.shape[0] // 4
    width = wbuf.shape[1]
    wait_all(start_rows(down_plan(rows), pieces, where_ref, rows, wbuf, sems, 0))
    glow = glow_ref[...]
    for j in range(4):
        grad = dot_nt(glow, wbuf[j * rows : (j + 1) * rows, :]) * slope_ref[j]
        low = grad.astype(bf16)
        guis[j][...] = low
        sm_ref[j : j + 1, :] = column_sum(low.astype(f32))
    sm_ref[4:8, :] = jnp.zeros((4, rows), f32)


def norm_back_kernel(where_ref, gsec_ref, n1_ref, inv_ref, vec_ref, *refs):
    guis, pieces, attn_pieces = refs[:4], refs[4:12], refs[12:18]
    gres_ref, gbr_ref, gatt_ref, sm_ref, wbuf, obuf, sems = refs[18:]
    rows = wbuf.shape[0] // 4
    hidden = wbuf.shape[1]
    width = obuf.shape[1]
    copies = start_rows(up_plan(rows), pieces, where_ref, rows, wbuf, sems, 0)
    out_copies = start_rows(attn_plan(rows, rows), attn_pieces, where_ref, rows, obuf, sems, 8)
    wait_all(copies)
    block = hidden // 4
    grad_normed = gsec_ref[...]
    for j in range(4):
        grad_normed = grad_normed + dot_nt(guis[j][...], wbuf[:, j * block : (j + 1) * block])
    normal = n1_ref[...]
    grad = norm_backward(grad_normed, normal, inv_ref[:, 0:1], vec_ref[G1 : G1 + 1, :])
    gres_ref[...] = grad
    low = grad.astype(bf16)
    gbr_ref[...] = low
    sm_ref[0:1, :] = column_sum(grad_normed * normal)
    sm_ref[1:2, :] = column_sum(grad_normed)
    sm_ref[2:3, :] = column_sum(low.astype(f32))
    sm_ref[3:8, :] = jnp.zeros((5, width), f32)
    wait_all(out_copies)
    gatt_ref[...] = dot_nt(low, obuf[...]).astype(bf16)


def attend_back_kernel(q_ref, k_ref, v_ref, gatt_ref, ids_ref, gq_ref, gk_ref, gv_ref, *, length):
    tokens, width = q_ref.shape
    cells = tokens // length
    scale = HEAD_DIM ** (-0.5)
    pair = 2 * HEAD_DIM
    masks = [head_mask(h, length) for h in range(2)]
    for c in range(cells):
        at = slice(c * length, (c + 1) * length)
        dead = jnp.broadcast_to(ids_ref[c : c + 1, :], (length, length)) == 0
        for p in range(width // pair):
            cols = slice(p * pair, (p + 1) * pair)
            q_pair, k_pair, v_pair = q_ref[at, cols], k_ref[at, cols], v_ref[at, cols]
            g_pair = gatt_ref[at, cols]
            zero = jnp.zeros_like(q_pair)
            gq = gk = gv = jnp.zeros((length, pair), f32)
            for h in range(2):
                mask = masks[h]
                soft = soft_rows(q_pair, k_pair, dead, mask)
                g_head = jnp.where(mask, g_pair, zero)
                grad_soft = dot_nt(g_head, v_pair)
                inner = jnp.sum(soft * grad_soft, axis=-1, keepdims=True)
                grad_scores = (soft * (grad_soft - inner)).astype(bf16)
                gv = gv + dot_tn(soft.astype(bf16), g_head)
                gq = gq + dot(grad_scores, jnp.where(mask, k_pair, zero))
                gk = gk + dot_tn(grad_scores, jnp.where(mask, q_pair, zero))
            gq_ref[at, cols] = (gq * scale).astype(bf16)
            gk_ref[at, cols] = (gk * scale).astype(bf16)
            gv_ref[at, cols] = gv.astype(bf16)


def input_back_kernel(
    where_ref, species_ref, gres_ref, gq_ref, gk_ref, gv_ref, sm2_ref, smu_ref, sm1_ref, *refs,
    length,
):
    pieces, later_pieces = refs[:6], refs[6:12]
    gin_ref, sm_ref, wbuf, sems = refs[12:]
    tokens, width = gres_ref.shape
    rows = width // 4
    copies = []
    for m in range(3):
        from_pieces = pieces if m < 2 else later_pieces
        plan = attn_plan((m % 2) * rows, rows)
        copies.append(start_rows(plan, from_pieces, where_ref, rows, wbuf.at[m], sems, 6 * m))
    sm_ref[BQ : BQ + 1, :] = column_sum(gq_ref[...].astype(f32))
    sm_ref[BV : BV + 1, :] = column_sum(gv_ref[...].astype(f32))
    sm_ref[BO : BO + 1, :] = sm1_ref[2:3, :]
    sm_ref[G1 : G1 + 2, :] = sm1_ref[0:2, :]
    sm_ref[BD : BD + 1, :] = sm2_ref[2:3, :]
    sm_ref[G2 : G2 + 2, :] = sm2_ref[0:2, :]
    sm_ref[BU : BU + 4, :] = smu_ref[0:4, :]
    sm_ref[BU + 4 : VEC_ROWS, :] = jnp.zeros((VEC_ROWS - BU - 4, width), f32)
    total = gres_ref[...]
    for m, grad in enumerate((gq_ref, gk_ref, gv_ref)):
        wait_all(copies[m])
        total = total + dot_nt(grad[...], wbuf[m])
    gin_ref[...] = total.astype(bf16)
    for s in range(2):
        row = jnp.zeros((1, width), f32)
        for c in range(tokens // length):
            cell = column_sum(total[c * length : (c + 1) * length, :])
            row = row + jnp.where(species_ref[c] == s, cell, jnp.zeros_like(cell))
        sm_ref[TB + s : TB + s + 1, :] = row


def half_rows(x, bit):
    rows = x.shape[-2] // 2
    return lax.dynamic_slice_in_dim(x, bit * rows, rows, x.ndim - 2)


def add(a, b):
    return (a.astype(f32) + b.astype(f32)).astype(bf16)


def two_way_chain(send_x, keep_x, send_b, keep_b, dp_index, bits, steps, b_first):
    p, q = [(dp_index >> bit) & 1 for bit in bits]
    one, two = [1 << bit for bit in bits]
    got_x = swap(send_x, "fsdp", 2)
    got_b = swap(send_b, "dp", one)
    last = send_b
    for over_x in (False, True) if b_first else (True, False):
        if over_x:
            got_x = yield got_x, last
            last = jnp.where(p == 0, add(keep_x[1], got_x[1]), add(keep_x[0], got_x[0]))
            take = jnp.where(p == 0, add(keep_x[0], got_x[0]), add(keep_x[1], got_x[1]))
            got_take = swap(last, "dp", one)
        else:
            got_b = yield got_b, last
            last = add(keep_b[1], got_b[1])
            rest = add(keep_b[0], got_b[0])
            got_rest = swap(last, "fsdp", 2)
    got_take = yield got_take, last
    first = add(take, got_take)
    got_rest = yield got_rest, first
    second = add(rest, got_rest)
    send = jnp.where(q == 0, second, first)
    keep = jnp.where(q == 0, first, second)
    got = yield swap(send, "dp", two), send
    total = add(keep, got)
    for step in steps[:-1]:
        bit = (dp_index >> step) & 1
        send = half_rows(total, 1 - bit)
        got = yield swap(send, "dp", 1 << step), send
        total = add(half_rows(total, bit), got)
    got = yield swap(total, "dp", 1 << steps[-1]), total
    total = add(total, got)
    for step in reversed(steps[:-1]):
        other = yield swap(total, "dp", 1 << step), total
        total = join_rows(total, other, dp_index, step)
    other = yield swap(total, "dp", two), total
    mine = jnp.stack([jnp.where(q == 0, total, other), jnp.where(q == 0, other, total)])
    other = yield swap(mine, "dp", one), mine
    return jnp.where(p == 0, mine, other), jnp.where(p == 0, other, mine)


def join_rows(total, other, dp_index, step):
    return jnp.where(
        (dp_index >> step) & 1 == 0,
        jnp.concatenate([total, other], axis=0),
        jnp.concatenate([other, total], axis=0),
    )


def halving_chain(send, keep, dp_index, steps):
    got = yield swap(send, "dp", 1 << steps[0]), send
    for step in steps[1:-1]:
        bit = (dp_index >> step) & 1
        send = add(half_rows(keep, 1 - bit), half_rows(got, 1 - bit))
        keep = add(half_rows(keep, bit), half_rows(got, bit))
        got = yield swap(send, "dp", 1 << step), send
    total = add(keep, got)
    got = yield swap(total, "dp", 1 << steps[-1]), total
    total = add(total, got)
    for step in reversed(steps[:-1]):
        other = yield swap(total, "dp", 1 << step), total
        total = join_rows(total, other, dp_index, step)
    return total


def whole_chain(total, steps):
    for axis, distance in (("fsdp", 1), ("fsdp", 2)) + tuple(("dp", 1 << step) for step in steps):
        got = yield swap(total, axis, distance), total
        total = total + got
    return total


class Turns:
    def __init__(self):
        self.pending, self.done = {}, {}

    def add(self, name, chain):
        self.pending[name] = next(chain)[0], chain

    def take(self, names, token):
        for name in names:
            if name in self.pending:
                value, chain = self.pending[name]
                try:
                    value, token = chain.send(tie(value, token))
                    self.pending[name] = value, chain
                except StopIteration as stop:
                    self.done[name] = stop.value
                    del self.pending[name]
        return token


def local(
    inputs,
    species,
    gene_ids,
    cotangent,
    table,
    w_query,
    b_query,
    w_key,
    w_value,
    b_value,
    w_out,
    b_out,
    gain_one,
    shift_one,
    w_up,
    b_up,
    w_down,
    b_down,
    gain_two,
    shift_two,
):
    cells, length, width = inputs.shape
    tokens = cells * length
    rows = w_query.shape[0]
    hidden = w_up.shape[1]
    shard_hidden = w_down.shape[0]
    shards = lax.axis_size("fsdp")
    f = lax.axis_index("fsdp")
    d = lax.axis_index("dp")
    y_bit = d & 1
    where = jnp.stack([f, y_bit, (d >> 1) & 1]).astype(jnp.int32)
    order = tuple(range((lax.axis_size("dp") - 1).bit_length()))

    z_bit = (d >> 1) & 1
    first_own, second_own, first_half, second_half = call(
        pack_kernel,
        (
            sds((2 * rows + VEC_ROWS, width), bf16),
            sds((2 * rows, width), bf16),
            sds((2 * rows + VEC_ROWS, width // 2), bf16),
            sds((2 * rows, width // 2), bf16),
        ),
        1,
        6 + TB,
        0,
        [pltpu.VMEM((VEC_ROWS, width), f32)],
        "pack",
        resident=False,
        limit=LARGE_VMEM_LIMIT,
    )(
        where,
        w_query,
        w_key,
        w_value,
        w_out,
        b_query,
        b_value,
        b_out,
        gain_one,
        shift_one,
        b_down,
        gain_two,
        shift_two,
        table,
        b_up,
    )

    def relays(half, axis_bit):
        across = swap(half, "fsdp", 2)
        return across, swap(across, "dp", axis_bit)

    def with_core(across, relayed, when=None):
        if when is not None:
            across, relayed = tie(across, when), tie(relayed, when)
        return across, relayed, swap(across, "fsdp", 1), swap(relayed, "fsdp", 1)

    first = relays(first_half, 1)
    second = relays(tie(second_half, first_half), 1)
    up_top = relays(tie(half_columns(w_up[: rows // 2], z_bit), first[0]), 2)
    up_rest = swap(tie(w_up[rows // 2 :], first[0]), "fsdp", 2)
    attn_first = (first_own, swap(first_own, "fsdp", 1), *with_core(*first))
    attn_second = (second_own, swap(second_own, "fsdp", 1), *with_core(*second))
    attn_first = tuple(map(in_hbm, attn_first))
    attn_second = tuple(map(in_hbm, attn_second))
    down_core = swap(w_down, "fsdp", 1)
    up_core = swap(w_up, "fsdp", 1)
    top = shard_hidden // 2
    down_top = swap(tie(half_columns(w_down[:top], y_bit), up_top[0]), "fsdp", 2)
    down_rest = swap(tie(half_columns(w_down[top:], z_bit), up_top[0]), "fsdp", 2)

    x_rows = inputs.reshape(tokens, width)
    cot_rows = cotangent.reshape(tokens, width)
    flat_low = sds((tokens, width), bf16)
    flat = sds((tokens, width), f32)
    small = sds((8, width), f32)
    q, k, v, own_attn, share_attn, n1, inv1, low, low_own, low_share, vec = call(
        partial(attend_kernel, length=length),
        (
            flat_low,
            flat_low,
            flat_low,
            pltpu.HBM((4, tokens, rows), bf16),
            pltpu.HBM((4, tokens, rows), bf16),
            flat,
            sds((tokens, 128), f32),
            flat_low,
            pltpu.HBM((2, tokens, rows), bf16),
            pltpu.HBM((2, tokens, rows), bf16),
            sds((VEC_ROWS, width), f32),
        ),
        2,
        2,
        12,
        [
            pltpu.VMEM((4, width, width), bf16),
            pltpu.VMEM((4 * VEC_ROWS, width), bf16),
            pltpu.VMEM((tokens, width), bf16),
            pltpu.VMEM((4, tokens, rows), bf16),
            pltpu.SemaphoreType.DMA((30,)),
        ],
        "attend",
        ATTEND_COST,
    )(where, species, x_rows, gene_ids, *attn_first, *attn_second)
    up_late = tie(up_rest, q)
    up = (w_up, up_core, *with_core(*up_top, q), up_late, swap(up_late, "fsdp", 1))
    down_top = tie(down_top, q)
    down_top = (down_top, swap(down_top, "dp", 1))
    act, act_own, act_near, act_across, slope = call(
        up_kernel,
        (
            sds((shards, tokens, shard_hidden), bf16),
            *(pltpu.HBM((tokens, shard_hidden), bf16),) * 2,
            pltpu.HBM((2, tokens, shard_hidden), bf16),
            sds((shards, tokens, shard_hidden), f32),
        ),
        1,
        2,
        8,
        [pltpu.VMEM((width, hidden), bf16), pltpu.SemaphoreType.DMA((8,))],
        "up",
    )(where, low, vec, *up)
    down_rest = tie(down_rest, act_own)
    down_rest = (down_rest, swap(down_rest, "dp", 2))
    down = (w_down, down_core, *with_core(*down_top, act_own), *with_core(*down_rest))
    output, gsec, glow, sm2 = call(
        down_kernel,
        (flat_low, flat, flat_low, small),
        1,
        4,
        10,
        [pltpu.VMEM((hidden, width), bf16), pltpu.SemaphoreType.DMA((10,))],
        "down",
    )(where, act, n1, vec, cot_rows, *down)
    act_got = swap(act_across, "fsdp", 2)
    glow_across = swap(glow, "fsdp", 2)
    *guis, smu = call(
        hidden_back_kernel,
        (*(sds((tokens, shard_hidden), bf16),) * 4, sds((8, shard_hidden), f32)),
        1,
        2,
        10,
        [pltpu.VMEM((hidden, width), bf16), pltpu.SemaphoreType.DMA((10,))],
        "hidden_back",
    )(where, glow, slope, *down)
    guis_got = [swap(part, "fsdp", 1) for part in guis]
    gres, gbr, gatt, sm1 = call(
        norm_back_kernel,
        (pltpu.HBM(flat.shape, f32), flat_low, flat_low, small),
        1,
        8,
        14,
        [
            pltpu.VMEM((width, hidden), bf16),
            pltpu.VMEM((width, width), bf16),
            pltpu.SemaphoreType.DMA((14,)),
        ],
        "norm_back",
    )(where, gsec, n1, inv1, vec, *guis, *up, *attn_second)
    part = pltpu.HBM((2, rows // 4, hidden), bf16)
    up_parts = call(near_up_kernel, (part,) * 4, 1, 10, 0, [], "near_up", resident=False)(
        tie(where, gbr), in_hbm(low_own), in_hbm(swap(low_share, "fsdp", 1)), *guis, *guis_got
    )
    gq, gk, gv = call(
        partial(attend_back_kernel, length=length),
        (flat_low, flat_low, flat_low),
        0,
        5,
        0,
        [],
        "attend_back",
    )(q, k, v, tie(gatt, up_parts[0]), gene_ids)
    act_all = (
        act_own,
        swap(tie(act_near, gbr), "fsdp", 1),
        act_got,
        swap(tie(act_got, gbr)[1], "fsdp", 1),
    )
    glow_all = (
        glow,
        swap(tie(glow, gbr), "fsdp", 1),
        glow_across,
        swap(tie(glow_across, gq), "fsdp", 1),
    )
    turns = Turns()
    turns.add("U", two_way_chain(*up_parts, d, UP_BITS, order[2:], UP_STRIPS_FIRST))
    rights = [gbr, gv, gq, gk]
    rights_got = [swap(right, "fsdp", 1) for right in rights]
    down_half = pltpu.HBM((shard_hidden // 2, width), bf16)
    send_down, keep_down = call(down_grad_kernel, (down_half,) * 2, 1, 8, 0, [], "down_grad", resident=False)(
        tie(where, gq), *map(in_hbm, act_all), glow, *map(in_hbm, glow_all[1:])
    )
    turns.add("D", halving_chain(send_down, keep_down, d, DOWN_BITS + order[2:]))
    token = turns.take(EARLY_TURNS, keep_down)
    pair = pltpu.HBM((2, rows, width), bf16)
    attn_parts = call(near_attn_kernel, (pair,) * 4, 1, 10, 0, [], "near_attn", resident=False)(
        tie(where, keep_down, token), in_hbm(own_attn), in_hbm(swap(share_attn, "fsdp", 1)), *rights, *map(in_hbm, rights_got)
    )
    turns.add("A", two_way_chain(*attn_parts, d, (0, 1), order[2:], False))
    token = turns.take(MIDDLE_TURNS, attn_parts[0])
    gin, sm = call(
        partial(input_back_kernel, length=length),
        (flat_low, sds((VEC_ROWS, width), f32)),
        2,
        7,
        12,
        [pltpu.VMEM((3, width, width), bf16), pltpu.SemaphoreType.DMA((18,))],
        "input_back",
        resident=False,
    )(
        tie(where, token),
        species,
        gres,
        gq,
        gk,
        gv,
        sm2,
        smu,
        sm1,
        *attn_first,
        *attn_second,
    )
    turns.add("S", whole_chain(sm, order))
    token = turns.take(TURNS, token)
    while turns.pending:
        token = turns.take(tuple(turns.pending), token)
    grad_up = jnp.stack(turns.done["U"]).reshape(rows, hidden)
    grad_down = turns.done["D"]
    low_attn, high_attn = turns.done["A"]
    sm = turns.done["S"]

    mine = lax.dynamic_slice_in_dim(sm, f * rows, rows, 1)
    b_up_grad = lax.dynamic_slice_in_dim(sm, BU + f, 1, 0)[0]

    return (
        output.reshape(inputs.shape),
        gin.reshape(inputs.shape),
        mine[TB : TB + 2],
        low_attn[1].astype(f32),
        mine[BQ],
        high_attn[1].astype(f32),
        high_attn[0].astype(f32),
        mine[BV],
        low_attn[0].astype(f32),
        mine[BO],
        mine[G1],
        mine[S1],
        grad_up.astype(f32),
        b_up_grad,
        grad_down.astype(f32),
        mine[BD],
        mine[G2],
        mine[S2],
    )


def solution(mesh):
    cells = P(("dp", "fsdp"), None, None)
    vector = P("fsdp")
    matrix = P("fsdp", None)
    table = P(None, "fsdp")
    return jax.shard_map(
        local,
        mesh=mesh,
        in_specs=(
            cells,
            P(("dp", "fsdp")),
            P(("dp", "fsdp"), None),
            cells,
            table,
            matrix,
            vector,
            matrix,
            matrix,
            vector,
            matrix,
            vector,
            vector,
            vector,
            matrix,
            vector,
            matrix,
            vector,
            vector,
            vector,
        ),
        out_specs=(
            cells,
            cells,
            table,
            matrix,
            vector,
            matrix,
            matrix,
            vector,
            matrix,
            vector,
            vector,
            vector,
            matrix,
            vector,
            matrix,
            vector,
            vector,
            vector,
        ),
        check_vma=False,
    )
```
